1024 devices in a mesh: seq: 64 (over z, y), heads: 8 (over x), dp: 2 (over core).
Axes of the slice: x: 8, y: 8, z: 8, core: 2. Of those that a mesh axis runs over, the one named last changes fastest.
Arguments:
- queries: bfloat16 [16384, 4096], P(('dp', 'seq'), 'heads'), parts along dimension 0, may hold values from -7 to 7
- keys: bfloat16 [16384, 4096], P(('dp', 'seq'), 'heads'), parts along dimension 0, may hold values from -7 to 7
- values: bfloat16 [16384, 4096], P(('dp', 'seq'), 'heads'), parts along dimension 0, may hold values from -6 to 6
- out_grad: bfloat16 [16384, 4096], P(('dp', 'seq'), 'heads'), parts along dimension 0, may hold values from -6 to 6
- random_blocks: int32 [64, 3, 128], P(('dp', 'heads')), parts along dimension 0, may hold values from 0 to 127, as said below
- global_blocks: int32 [4], P('dp'), parts along dimension 0, may hold values from 0 to 127
Outputs:
- attended: bfloat16 [16384, 4096], P(('dp', 'seq'), 'heads'), parts along dimension 0
- query_grad: bfloat16 [16384, 4096], P(('dp', 'seq'), 'heads'), parts along dimension 0
- key_grad: bfloat16 [16384, 4096], P(('dp', 'seq'), 'heads'), parts along dimension 0
- value_grad: bfloat16 [16384, 4096], P(('dp', 'seq'), 'heads'), parts along dimension 0
The draws below stay inside these ranges and needn't reach their ends.
There are 2 independent parts, one for each index of `dp`. The reference program is written for one: setup_inputs(seed, part) draws one part's arguments, and reference() takes and returns one part's arrays. A program takes and returns all parts, laid end to end along the dimension named above; each array names one. Nothing has to cross between parts.
Inputs may be any that keep to these rules, and one draw needn't show every extreme that they name: `random_blocks`: entries are key block numbers. Among the entries of the 2 query blocks of one index of seq and the 4 heads of one index of heads, at most 1 name blocks of the same index of seq (block // 2), and some index of seq is named exactly 1 times.
All inputs are finite; a program needn't handle non-finite values.
Results may differ from the reference program's by a relative error of at most 0.024.
Values may be sent and summed in bfloat16 or wider, within the bound.
A program may use at most 32 MiB of HBM per device.

```python
import jax
import jax.numpy as jnp
from jax import lax

HEADS = 32
HD = 128
BLK = 64
NRAND = 3
NGLOB = 2
QB_DEV = 2
SEQ = 8192
NB = 128
HEADS_DEV = 4
CAP = 1


def draw_queries(key, part):
    base = jnp.clip(jax.random.normal(jax.random.fold_in(key, 11), (SEQ, HEADS * HD), jnp.float32), -6.0, 6.0)
    return base.astype(jnp.bfloat16)


def draw_keys(key, part):
    base = jnp.clip(jax.random.normal(jax.random.fold_in(key, 12), (SEQ, HEADS * HD), jnp.float32), -6.0, 6.0)
    return base.astype(jnp.bfloat16)


def draw_random_blocks(key, part):
    seq_groups = NB // QB_DEV
    head_groups = HEADS // HEADS_DEV
    group_count = seq_groups * head_groups
    item_count = QB_DEV * HEADS_DEV * NRAND
    group_keys = jax.random.split(jax.random.fold_in(key, 21), group_count)
    orders = jax.vmap(lambda single: jax.random.permutation(single, seq_groups * CAP))(group_keys)
    owners = orders[:, :item_count] // CAP
    within = jax.random.randint(jax.random.fold_in(key, 22), (group_count, item_count), 0, QB_DEV)
    picked = (owners * QB_DEV + within).reshape(seq_groups, head_groups, QB_DEV, HEADS_DEV, NRAND)
    return picked.transpose(1, 3, 4, 0, 2).reshape(HEADS, NRAND, NB).astype(jnp.int32)


def block_scale(own_key, extent, pieces, least, high):
    level, own = 1.0, jax.random.fold_in(own_key, 6)
    for position, blocks in pieces:
        draws = jnp.exp(jax.random.uniform(jax.random.fold_in(own, position), (blocks,), jnp.float32, least / len(pieces), high / len(pieces)))
        level = level * jnp.repeat(draws, extent[position] // blocks).reshape([-1 if axis == position else 1 for axis in range(len(extent))])
    return level


def centred(key, dims, scale, reach, pieces=(), kind=jnp.bfloat16):
    loudness = block_scale(key, dims, pieces, -0.22, 0.18) if pieces else 1.0
    values = jax.random.normal(key, dims, jnp.float32) * scale * loudness
    return jnp.minimum(jnp.maximum(values, -reach), reach).astype(kind)


def setup_inputs(seed: int = 0, part: int = 0) -> dict:
    arg_keys = jax.random.split(jax.random.key(seed), 7)
    part_keys = jax.random.split(jax.random.fold_in(arg_keys[6], part), 7)
    queries = draw_queries(jax.random.fold_in(jax.random.fold_in(arg_keys[6], part), 71), part)
    keys = draw_keys(jax.random.fold_in(jax.random.fold_in(arg_keys[6], part), 71), part)
    values = centred(part_keys[2], (SEQ, HEADS * HD), 1.0, 6.0, ((0, 64), (1, 8)))
    out_grad = centred(part_keys[3], (SEQ, HEADS * HD), 1.0, 6.0, ((0, 64), (1, 8)))
    random_blocks = draw_random_blocks(jax.random.fold_in(jax.random.fold_in(arg_keys[6], part), 71), part)
    global_blocks = jax.random.randint(part_keys[5], (NGLOB,), 0, NB).astype(jnp.int32)
    return {"queries": queries, "keys": keys, "values": values, "out_grad": out_grad, "random_blocks": random_blocks, "global_blocks": global_blocks}


def reference(queries, keys, values, out_grad, random_blocks, global_blocks):
    score_scale = HD ** -0.5
    full_width = HEADS * HD
    slot_count = 3 + NRAND + NGLOB

    def heads_first(tensor):
        return tensor.reshape(NB, BLK, HEADS, HD).transpose(2, 0, 1, 3)

    def restore(tensor):
        return tensor.transpose(1, 2, 0, 3).reshape(NB * BLK, full_width)

    block_ids = jnp.arange(NB, dtype=jnp.int32)
    left_ids = jnp.maximum(block_ids - 1, 0).astype(jnp.int32)
    right_ids = jnp.minimum(block_ids + 1, NB - 1).astype(jnp.int32)
    glob_ids = jnp.broadcast_to(global_blocks.astype(jnp.int32)[None, :], (NB, NGLOB))
    always = jnp.ones((NB,), dtype=bool)
    slot_valid = jnp.stack([block_ids >= 1, always, block_ids <= NB - 2] + [always] * (NRAND + NGLOB), 1)
    row_valid = jnp.repeat(slot_valid, BLK, axis=1)

    def gather_terms(parts, key_index):
        random_part = lax.optimization_barrier(parts[:, 3:3 + NRAND].astype(jnp.bfloat16)).astype(jnp.float32)
        joined = jnp.concatenate([parts[:, :3], random_part, parts[:, 3 + NRAND:]], 1)
        total = jnp.zeros((NB, BLK, HD), jnp.float32).at[key_index.reshape(-1)].add(joined.reshape(-1, BLK, HD))
        return total.astype(jnp.bfloat16)

    def one_head(operands):
        query_head, key_head, value_head, grad_head, random_head = operands
        random_rows = random_head.transpose(1, 0).astype(jnp.int32)
        key_index = jnp.concatenate([left_ids[:, None], block_ids[:, None], right_ids[:, None], random_rows, glob_ids], 1)
        query_f = query_head.astype(jnp.float32)
        grad_f = grad_head.astype(jnp.float32)
        key_list = key_head[key_index].reshape(NB, slot_count * BLK, HD).astype(jnp.float32)
        value_list = value_head[key_index].reshape(NB, slot_count * BLK, HD).astype(jnp.float32)
        scores = jnp.einsum("nqd,nkd->nqk", query_f, key_list) * score_scale
        scores = jnp.where(row_valid[:, None, :], scores, -jnp.inf)
        row_max = jnp.max(scores, -1, keepdims=True)
        log_total = row_max + jnp.log(jnp.sum(jnp.exp(scores - row_max), -1, keepdims=True))
        probs = jnp.exp(scores - log_total)
        probs_low = probs.astype(jnp.bfloat16)
        attended = jnp.einsum("nqk,nkd->nqd", probs_low.astype(jnp.float32), value_list).astype(jnp.bfloat16)
        delta_rows = jnp.sum(grad_f * attended.astype(jnp.float32), -1, keepdims=True)
        prob_grad = jnp.einsum("nqd,nkd->nqk", grad_f, value_list)
        score_grad = (score_scale * probs * (prob_grad - delta_rows)).astype(jnp.bfloat16)
        query_grad = jnp.einsum("nqk,nkd->nqd", score_grad.astype(jnp.float32), key_list).astype(jnp.bfloat16)
        key_parts = jnp.einsum("nqk,nqd->nkd", score_grad.astype(jnp.float32), query_f).reshape(NB, slot_count, BLK, HD)
        value_parts = jnp.einsum("nqk,nqd->nkd", probs_low.astype(jnp.float32), grad_f).reshape(NB, slot_count, BLK, HD)
        return attended, query_grad, gather_terms(key_parts, key_index), gather_terms(value_parts, key_index)

    results = lax.map(one_head, (heads_first(queries), heads_first(keys), heads_first(values), heads_first(out_grad), random_blocks))
    return (restore(results[0]), restore(results[1]), restore(results[2]), restore(results[3]))
```

```python
import jax
import jax.numpy as jnp
from jax import lax
from jax.experimental import pallas as pl
from jax.experimental.pallas import tpu as pltpu
from jax.sharding import PartitionSpec as P

MESH = pl.DeviceIdType.MESH
BLK = 64
HD = 128
N = 8
HEADS = 4
NRAND = 3
NGLOB = 2
ITEMS = 2 * HEADS
CODE_K, CODE_V, INV, SRC, GLB = 0, 64, 128, 192, 216
SLOTS = N + 1
F32 = jnp.float32
BF16 = jnp.bfloat16
ROWS_T = (((1,), (1,)), ((), ()))
COLS_T = (((0,), (0,)), ((), ()))

AG = [(dr, s, c) for s in range(1, 5) for c in (0, 1) for dr in (1, -1) if s < 4 or (dr == 1) == (c == 0)]
FLOWS = [(1, 0, 4), (-1, 1, 4), (1, 1, 3), (-1, 0, 3)]
RS = [(f, s) for s in range(1, 5) for f in range(4) if s <= FLOWS[f][2]]


def kernel(
    tab, q, k, v, g,
    att, dq, dk, dv,
    agk, agv, wink, winv, sk, sv, rk, rv, gk, gv,
    ka, va, termk, termv, wk, wv, gak, gav, hsk, hsv, hrk, hrv,
    rsk, rsv, rrk, rrv, pk, pv, g2k, g2v, g3k, g3v,
    rsend, rrecv,
    lsem, ag_s, ag_r, h_s, h_r, b_s, b_r, gg_s, gg_r,
    hb_s, hb_r, rb_s, rb_r, g2_s, g2_r, g3_s, g3_r, rs_s, rs_r,
):
    me = lax.axis_index("seq")
    z = me // N
    y = me % N
    total = N * N

    def dev(axis, off):
        if axis == "y":
            return z * N + (y + off + N) % N
        return ((z + off + N) % N) * N + y

    pos = {"y": y, "z": z}

    def rc(src, dst, ss, rs, to):
        return pltpu.make_async_remote_copy(
            src_ref=src, dst_ref=dst, send_sem=ss, recv_sem=rs, device_id={"seq": to}, device_id_type=MESH
        )

    locals_ = []
    for i in range(ITEMS):
        part_of = (pl.ds(i // HEADS * BLK, BLK), pl.ds(i % HEADS * HD, HD))
        locals_.append(pltpu.make_async_copy(k.at[part_of], agk.at[y, i], lsem.at[i]))
        locals_.append(pltpu.make_async_copy(v.at[part_of], agv.at[z, i], lsem.at[ITEMS + i]))
    win_own = [
        pltpu.make_async_copy(k, wink.at[pl.ds(BLK, 2 * BLK)], lsem.at[2 * ITEMS]),
        pltpu.make_async_copy(v, winv.at[pl.ds(BLK, 2 * BLK)], lsem.at[2 * ITEMS + 1]),
    ]
    for c in locals_ + win_own:
        c.start()

    barrier = pltpu.get_barrier_semaphore()
    right_seq = (me + 1) % total
    left_seq = (me + total - 1) % total

    def greet(d, carry):
        pl.semaphore_signal(barrier, inc=1, device_id={"seq": dev("y", d)}, device_id_type=MESH)
        pl.semaphore_signal(barrier, inc=1, device_id={"seq": dev("z", d)}, device_id_type=MESH)
        return carry

    lax.fori_loop(1, N, greet, 0)
    pl.semaphore_signal(barrier, inc=1, device_id={"seq": right_seq}, device_id_type=MESH)
    pl.semaphore_signal(barrier, inc=1, device_id={"seq": left_seq}, device_id_type=MESH)
    for c in locals_:
        c.wait()
    pl.semaphore_wait(barrier, 2 * N)

    def ag_copy(arr, i):
        dr, s, c = AG[i]
        axis, buf = (("y", agk), ("z", agv))[arr]
        slot = (pos[axis] - dr * (s - 1) + N) % N
        rows = pl.ds(c * HEADS, HEADS)
        return rc(buf.at[slot, rows], buf.at[slot, rows], ag_s.at[arr, i], ag_r.at[arr, i], dev(axis, dr))

    def ag_wait(arr, i):
        dr, s, c = AG[i]
        axis, buf = (("y", agk), ("z", agv))[arr]
        slot = (pos[axis] - dr * s + N) % N
        rows = pl.ds(c * HEADS, HEADS)
        rc(buf.at[slot, rows], buf.at[slot, rows], ag_s.at[arr, i], ag_r.at[arr, i], dev(axis, dr)).wait_recv()

    index = {key: i for i, key in enumerate(AG)}
    for i, (dr, s, c) in enumerate(AG):
        if s == 1:
            for arr in (0, 1):
                ag_copy(arr, i).start()

    halo = [
        rc(k.at[pl.ds(BLK, BLK)], wink.at[pl.ds(0, BLK)], h_s.at[0], h_r.at[0], right_seq),
        rc(v.at[pl.ds(BLK, BLK)], winv.at[pl.ds(0, BLK)], h_s.at[1], h_r.at[1], right_seq),
        rc(k.at[pl.ds(0, BLK)], wink.at[pl.ds(3 * BLK, BLK)], h_s.at[2], h_r.at[2], left_seq),
        rc(v.at[pl.ds(0, BLK)], winv.at[pl.ds(3 * BLK, BLK)], h_s.at[3], h_r.at[3], left_seq),
    ]

    for i, (dr, s, c) in enumerate(AG):
        for arr in (0, 1):
            ag_wait(arr, i)
            nxt = index.get((dr, s + 1, c))
            if nxt is not None:
                ag_copy(arr, nxt).start()
        if i == 3:
            for c_ in halo:
                c_.start()
    for c in win_own:
        c.wait()

    def item(buf, slot, code):
        return buf[slot, code]

    gblk = [tab[GLB + i] for i in range(NGLOB)]

    def pick(idx):
        return jnp.where(idx // HEADS == 0, gblk[0], gblk[1])

    def far_first(j):
        return jnp.where(j % 2 == 1, N // 2 - (j + 1) // 2, N // 2 + j // 2)

    def fill(dst_k, dst_v, zd, yd):
        for s in range(N):
            dst_k[s] = item(agk, s, jnp.maximum(tab[CODE_K + zd * N + s], 0))
            dst_v[s] = item(agv, s, jnp.maximum(tab[CODE_V + yd * N + s], 0))
        blk = pick(y)
        dst_k[N] = item(agk, blk // 2 % N, blk % 2 * HEADS + y % HEADS)
        blk = pick(z)
        dst_v[N] = item(agv, blk // (2 * N), blk % 2 * HEADS + z % HEADS)

    def bundle(j, carry):
        d = far_first(j)
        zd = (z + d) % N
        yd = (y + d) % N
        fill(sk.at[j], sv.at[j], zd, yd)
        rc(sk.at[j], rk.at[z], b_s.at[0, j], b_r.at[0, j], zd * N + y).start()
        rc(sv.at[j], rv.at[y], b_s.at[1, j], b_r.at[1, j], z * N + yd).start()
        return carry

    lax.fori_loop(0, N - 1, bundle, 0)
    fill(rk.at[z], rv.at[y], z, y)

    def bundle_wait(j, carry):
        d = far_first(j)
        zs = (z + N - d) % N
        ys = (y + N - d) % N
        rc(sk.at[j], rk.at[zs], b_s.at[0, j], b_r.at[0, j], zs * N + y).wait_recv()
        rc(sv.at[j], rv.at[ys], b_s.at[1, j], b_r.at[1, j], z * N + ys).wait_recv()
        return carry

    lax.fori_loop(0, N - 1, bundle_wait, 0)

    gk[y] = rk[pick(y) // (2 * N), N]
    gv[z] = rv[pick(z) // 2 % N, N]

    def small(src_k, src_v, ss, rs, axis_k, axis_v):
        def start(j, carry):
            d = j + 1
            rc(src_k.at[pos[axis_k]], src_k.at[pos[axis_k]], ss.at[0, j], rs.at[0, j], dev(axis_k, d)).start()
            rc(src_v.at[pos[axis_v]], src_v.at[pos[axis_v]], ss.at[1, j], rs.at[1, j], dev(axis_v, d)).start()
            return carry

        lax.fori_loop(0, N - 1, start, 0)

    def small_wait(src_k, src_v, ss, rs, axis_k, axis_v):
        def wait(j, carry):
            d = N - 1 - j
            sl = (pos[axis_k] + d) % N
            rc(src_k.at[sl], src_k.at[sl], ss.at[0, j], rs.at[0, j], dev(axis_k, d)).wait_recv()
            sl = (pos[axis_v] + d) % N
            rc(src_v.at[sl], src_v.at[sl], ss.at[1, j], rs.at[1, j], dev(axis_v, d)).wait_recv()
            return carry

        lax.fori_loop(0, N - 1, wait, 0)

    small(gk, gv, gg_s, gg_r, "y", "z")
    for c_ in halo:
        c_.wait_recv()
    small_wait(gk, gv, gg_s, gg_r, "y", "z")

    scale = HD ** (-0.5)
    key_count = (3 + NRAND + NGLOB) * BLK

    def head(h, carry):
        cols = pl.ds(pl.multiple_of(h * HD, HD), HD)
        for b in range(2):
            rows = pl.ds(b * BLK, BLK)
            kb, vb = ka.at[b], va.at[b]
            kb[pl.ds(0, 3 * BLK)] = wink[pl.ds(b * BLK, 3 * BLK), cols]
            vb[pl.ds(0, 3 * BLK)] = winv[pl.ds(b * BLK, 3 * BLK), cols]
            for r in range(NRAND):
                src = tab[SRC + (h * NRAND + r) * 2 + b] // 2
                kb[pl.ds((3 + r) * BLK, BLK)] = rk[src // N, src % N]
                vb[pl.ds((3 + r) * BLK, BLK)] = rv[src % N, src // N]
            for gi in range(NGLOB):
                kb[pl.ds((6 + gi) * BLK, BLK)] = gk[gi * HEADS + h]
                vb[pl.ds((6 + gi) * BLK, BLK)] = gv[gi * HEADS + h]
            kall, vall = kb[...], vb[...]
            qb, gb = q[rows, cols], g[rows, cols]
            s = lax.dot_general(qb, kall, ROWS_T, preferred_element_type=F32) * scale
            key_id = lax.broadcasted_iota(jnp.int32, (BLK, key_count), 1)
            if b == 0:
                bad = (key_id < BLK) & (me == 0)
            else:
                bad = (key_id >= 2 * BLK) & (key_id < 3 * BLK) & (me == total - 1)
            s = jnp.where(bad, -jnp.inf, s)
            m = jnp.max(s, -1, keepdims=True)
            e = jnp.exp(s - m)
            p = e * (1.0 / jnp.sum(e, -1, keepdims=True))
            plow = p.astype(BF16)
            o = lax.dot_general(plow, vall, (((1,), (0,)), ((), ())), preferred_element_type=F32).astype(BF16)
            delta = jnp.sum(gb.astype(F32) * o.astype(F32), -1, keepdims=True)
            dp = lax.dot_general(gb, vall, ROWS_T, preferred_element_type=F32)
            ds = (scale * p * (dp - delta)).astype(BF16)
            att[rows, cols] = o
            dq[rows, cols] = lax.dot_general(
                ds, kall, (((1,), (0,)), ((), ())), preferred_element_type=F32
            ).astype(BF16)
            for lhs, rhs, win, term, gacc in ((ds, qb, wk, termk, gak), (plow, gb, wv, termv, gav)):
                t = lax.dot_general(lhs, rhs, COLS_T, preferred_element_type=F32)
                if b == 0:
                    win[pl.ds(0, 3 * BLK), cols] = t[: 3 * BLK]
                else:
                    win[pl.ds(BLK, 2 * BLK), cols] += t[: 2 * BLK]
                    win[pl.ds(3 * BLK, BLK), cols] = t[2 * BLK : 3 * BLK]
                for r in range(NRAND):
                    term[(h * NRAND + r) * 2 + b] = t[(3 + r) * BLK : (4 + r) * BLK].astype(BF16)
                for gi in range(NGLOB):
                    piece = t[(6 + gi) * BLK : (7 + gi) * BLK]
                    if b == 0:
                        gacc[gi * HEADS + h] = piece
                    else:
                        gacc[gi * HEADS + h] += piece
        return carry

    lax.fori_loop(0, HEADS, head, 0)

    def fill_back(dst_k, dst_v, zd, yd):
        for s in range(N):
            dst_k[s] = termk[tab[INV + zd * N + s]]
            dst_v[s] = termv[tab[INV + s * N + yd]]
        dst_k[N] = gak[zd].astype(BF16)
        dst_v[N] = gav[yd].astype(BF16)

    hsk[0] = wk[pl.ds(0, BLK)].astype(BF16)
    hsk[1] = wk[pl.ds(3 * BLK, BLK)].astype(BF16)
    hsv[0] = wv[pl.ds(0, BLK)].astype(BF16)
    hsv[1] = wv[pl.ds(3 * BLK, BLK)].astype(BF16)

    def back(j, carry):
        d = far_first(j)
        zd = (z + d) % N
        yd = (y + d) % N
        fill_back(rsk.at[j], rsv.at[j], zd, yd)
        rc(rsk.at[j], rrk.at[z], rb_s.at[0, j], rb_r.at[0, j], zd * N + y).start()
        rc(rsv.at[j], rrv.at[y], rb_s.at[1, j], rb_r.at[1, j], z * N + yd).start()
        return carry

    lax.fori_loop(0, N - 1, back, 0)
    fill_back(rrk.at[z], rrv.at[y], z, y)
    halo_back = [
        rc(hsk.at[0], hrk.at[1], hb_s.at[0], hb_r.at[0], left_seq),
        rc(hsk.at[1], hrk.at[0], hb_s.at[1], hb_r.at[1], right_seq),
        rc(hsv.at[0], hrv.at[1], hb_s.at[2], hb_r.at[2], left_seq),
        rc(hsv.at[1], hrv.at[0], hb_s.at[3], hb_r.at[3], right_seq),
    ]
    for c_ in halo_back:
        c_.start()

    def back_wait(j, carry):
        d = far_first(j)
        zs = (z + N - d) % N
        ys = (y + N - d) % N
        rc(rsk.at[j], rrk.at[zs], rb_s.at[0, j], rb_r.at[0, j], zs * N + y).wait_recv()
        rc(rsv.at[j], rrv.at[ys], rb_s.at[1, j], rb_r.at[1, j], z * N + ys).wait_recv()
        return carry

    lax.fori_loop(0, N - 1, back_wait, 0)

    def total_of(read):
        acc = read(0).astype(F32)
        for s in range(1, N):
            acc += read(s).astype(F32)
        return acc.astype(BF16)

    g2k[y] = total_of(lambda s: rrk[s, N])
    g2v[z] = total_of(lambda s: rrv[s, N])
    small(g2k, g2v, g2_s, g2_r, "y", "z")

    tile = 16

    def partial(rel):
        for buf, part, base, p in ((rrk, pk, CODE_K, y), (rrv, pv, CODE_V, z)):
            tgt = (p + rel) % N
            weight = []
            for s in range(N):
                code = tab[base + s * N + tgt]
                weight.append([jnp.where(code == i, 1.0, 0.0).astype(F32) for i in range(ITEMS)])

            def rows_step(i, carry, buf=buf, part=part, tgt=tgt, weight=weight):
                rows = pl.ds(pl.multiple_of(i * tile, tile), tile)
                acc = [None] * ITEMS
                for s in range(N):
                    x = buf[s, tgt, rows].astype(F32)
                    for c in range(ITEMS):
                        w = x * weight[s][c]
                        acc[c] = w if acc[c] is None else acc[c] + w
                for c in range(ITEMS):
                    part[tgt, c, rows] = acc[c]
                return carry

            lax.fori_loop(0, BLK // tile, rows_step, 0)

    rs_index = {key: i for i, key in enumerate(RS)}

    def rs_copy(arr, i):
        f, s = RS[i]
        return rc(rsend.at[arr, i], rrecv.at[arr, i], rs_s.at[arr, i], rs_r.at[arr, i],
                  dev(("y", "z")[arr], FLOWS[f][0]))

    def rs_send(f, s):
        dr, c, hops = FLOWS[f]
        i = rs_index[(f, s)]
        for arr, part, p in ((0, pk, y), (1, pv, z)):
            tgt = (p + dr * (hops - s + 1) + N) % N
            x = part[tgt, pl.ds(c * HEADS, HEADS)]
            if s > 1:
                j = rs_index[(f, s - 1)]
                rs_copy(arr, j).wait_recv()
                x = x + rrecv[arr, j].astype(F32)
            rsend[arr, i] = x.astype(BF16)
            rs_copy(arr, i).start()

    def step_loop(first, stride, count):
        def body(j, carry):
            partial(first + stride * j)
            return carry

        lax.fori_loop(0, count, body, 0)

    step_loop(3, 1, 3)
    for f in range(4):
        rs_send(f, 1)
    step_loop(2, 4, 2)
    for f in range(4):
        rs_send(f, 2)
    small_wait(g2k, g2v, g2_s, g2_r, "y", "z")
    g3k[z] = total_of(lambda s: g2k[s])
    g3v[y] = total_of(lambda s: g2v[s])
    small(g3k, g3v, g3_s, g3_r, "z", "y")
    step_loop(0, 1, 2)
    step_loop(7, 1, 1)
    for f in range(4):
        rs_send(f, 3)
    for f in range(2):
        rs_send(f, 4)
    for c_ in halo_back:
        c_.wait_recv()
    small_wait(g3k, g3v, g3_s, g3_r, "z", "y")

    for f in (2, 3, 0, 1):
        for arr in (0, 1):
            rs_copy(arr, rs_index[(f, FLOWS[f][2])]).wait_recv()
    for arr, part, p, win, hr, g3, out in (
        (0, pk, y, wk, hrk, g3k, dk),
        (1, pv, z, wv, hrv, g3v, dv),
    ):
        for b in range(2):
            flows = [f for f in range(4) if FLOWS[f][1] == b]
            for h in range(HEADS):
                cols = pl.ds(h * HD, HD)
                x = win[pl.ds((1 + b) * BLK, BLK), cols] + hr[b, :, cols].astype(F32)
                x += part[p, b * HEADS + h]
                for f in flows:
                    x += rrecv[arr, rs_index[(f, FLOWS[f][2])], h].astype(F32)
                for gi in range(NGLOB):
                    mine = jnp.where(gblk[gi] == me * 2 + b, 1.0, 0.0).astype(F32)
                    x += g3[gi * HEADS + h].astype(F32) * mine
                out[pl.ds(b * BLK, BLK), cols] = x.astype(BF16)

    for arr in (0, 1):
        for i in range(len(AG)):
            ag_copy(arr, i).wait_send()
        for i in range(len(RS)):
            rs_copy(arr, i).wait_send()
    for c_ in halo + halo_back:
        c_.wait_send()

    def drain(j, carry):
        for a, (bk, bv) in ((b_s, (sk, sv)), (rb_s, (rsk, rsv))):
            rc(bk.at[j], rk.at[z], a.at[0, j], b_r.at[0, j], me).wait_send()
            rc(bv.at[j], rv.at[y], a.at[1, j], b_r.at[1, j], me).wait_send()
        for a, (bk, bv), (ik, iv) in (
            (gg_s, (gk, gv), (y, z)),
            (g2_s, (g2k, g2v), (y, z)),
            (g3_s, (g3k, g3v), (z, y)),
        ):
            rc(bk.at[ik], bk.at[ik], a.at[0, j], gg_r.at[0, j], me).wait_send()
            rc(bv.at[iv], bv.at[iv], a.at[1, j], gg_r.at[1, j], me).wait_send()
        return carry

    lax.fori_loop(0, N - 1, drain, 0)


def tables(random_blocks, global_blocks):
    me = lax.axis_index("seq")
    z, y = me // N, me % N
    lists = random_blocks.reshape(HEADS * NRAND, N, N, 2)
    head = (jnp.arange(HEADS * NRAND, dtype=jnp.int32) // NRAND)[:, None, None]
    span = jnp.arange(N, dtype=jnp.int32)

    def codes(rows, owner_ids):
        owner = rows // 2
        code = rows % 2 * HEADS + head + 1
        hit = owner[..., None] == owner_ids
        return jnp.sum(jnp.where(hit, code[..., None], 0), (0, 2)).reshape(N * N) - 1

    code_k = codes(lax.dynamic_index_in_dim(lists, y, 2, keepdims=False), z * N + span)
    code_v = codes(lax.dynamic_index_in_dim(lists, z, 1, keepdims=False), span * N + y)
    mine = lax.dynamic_index_in_dim(
        lax.dynamic_index_in_dim(lists, z, 1, keepdims=False), y, 1, keepdims=False
    ).reshape(HEADS * NRAND * 2)
    order = jnp.arange(HEADS * NRAND * 2, dtype=jnp.int32)
    hit = (mine // 2)[:, None] == jnp.arange(N * N, dtype=jnp.int32)[None, :]
    inv = jnp.sum(jnp.where(hit, order[:, None], 0), 0)
    return jnp.concatenate([code_k, code_v, inv, mine, global_blocks]).astype(jnp.int32)


def body(queries, keys, values, out_grad, random_blocks, global_blocks):
    tab = tables(random_blocks, global_blocks)
    full = jax.ShapeDtypeStruct(queries.shape, BF16)
    vm, dma = pltpu.VMEM, pltpu.SemaphoreType.DMA
    bund = lambda n: vm((n, SLOTS, BLK, HD), BF16)
    keys_n = (3 + NRAND + NGLOB) * BLK
    scratch = [
        vm((N, ITEMS, BLK, HD), BF16), vm((N, ITEMS, BLK, HD), BF16),
        vm((4 * BLK, HEADS * HD), BF16), vm((4 * BLK, HEADS * HD), BF16),
        bund(N - 1), bund(N - 1), bund(N), bund(N),
        vm((N, BLK, HD), BF16), vm((N, BLK, HD), BF16),
        vm((2, keys_n, HD), BF16), vm((2, keys_n, HD), BF16),
        vm((24, BLK, HD), BF16), vm((24, BLK, HD), BF16),
        vm((4 * BLK, HEADS * HD), F32), vm((4 * BLK, HEADS * HD), F32),
        vm((N, BLK, HD), F32), vm((N, BLK, HD), F32),
        vm((2, BLK, HEADS * HD), BF16), vm((2, BLK, HEADS * HD), BF16),
        vm((2, BLK, HEADS * HD), BF16), vm((2, BLK, HEADS * HD), BF16),
        bund(N - 1), bund(N - 1), bund(N), bund(N),
        vm((N, ITEMS, BLK, HD), F32), vm((N, ITEMS, BLK, HD), F32),
        vm((N, BLK, HD), BF16), vm((N, BLK, HD), BF16),
        vm((N, BLK, HD), BF16), vm((N, BLK, HD), BF16),
        vm((2, len(RS), HEADS, BLK, HD), BF16), vm((2, len(RS), HEADS, BLK, HD), BF16),
        dma((2 * ITEMS + 2,)), dma((2, len(AG))), dma((2, len(AG))), dma((4,)), dma((4,)),
        dma((2, N - 1)), dma((2, N - 1)), dma((2, N - 1)), dma((2, N - 1)),
        dma((4,)), dma((4,)), dma((2, N - 1)), dma((2, N - 1)),
        dma((2, N - 1)), dma((2, N - 1)), dma((2, N - 1)), dma((2, N - 1)),
        dma((2, len(RS))), dma((2, len(RS))),
    ]
    spec = pl.BlockSpec(memory_space=pltpu.VMEM)
    return pl.pallas_call(
        kernel,
        out_shape=(full,) * 4,
        in_specs=[pl.BlockSpec(memory_space=pltpu.SMEM)] + [spec] * 4,
        out_specs=(spec,) * 4,
        scratch_shapes=scratch,
        compiler_params=pltpu.CompilerParams(collective_id=0, has_side_effects=True),
    )(tab, queries, keys, values, out_grad)


def solution(mesh):
    wide = P(("dp", "seq"), "heads")
    return jax.shard_map(
        body,
        mesh=mesh,
        in_specs=(wide, wide, wide, wide, P(("dp", "heads"), None, None), P("dp")),
        out_specs=(wide,) * 4,
        check_vma=False,
    )
```

```python
import jax
import jax.numpy as jnp
from jax import lax
from jax.experimental import pallas as pl
from jax.experimental.pallas import tpu as pltpu
from jax.sharding import PartitionSpec as P

MESH = pl.DeviceIdType.MESH
BLK = 64
HD = 128
N = 8
HEADS = 4
NRAND = 3
NGLOB = 2
ITEMS = 2 * HEADS
F32 = jnp.float32
BF16 = jnp.bfloat16
ROWS_T = (((1,), (1,)), ((), ()))
COLS_T = (((0,), (0,)), ((), ()))

AG = [(dr, s, c) for s in range(1, 5) for c in (0, 1) for dr in (1, -1) if s < 4 or (dr == 1) == (c == 0)]
FLOWS = [(1, 0, 4), (-1, 1, 4), (1, 1, 3), (-1, 0, 3)]
RS = [(f, s) for s in range(1, 5) for f in range(4) if s <= FLOWS[f][2]]


def kernel(
    glb, lists, q_hbm, k, v, g_hbm,
    att, dq, dk, dv,
    q, g, rbv, rbs,
    tvm, tsm, gsk, gsv, gck, gcv,
    agk, agv, wink, winv, sk, sv, rk, rv, gk, gv,
    ka, va, termk, termv, wk, wv, gak, gav, hsk, hsv, hrk, hrv,
    rsk, rsv, rrk, rrv, pk, pv, g2k, g2v, g3k, g3v,
    rsend, rrecv,
    tsem, gc_s, gc_r, lsem, ag_s, ag_r, h_s, h_r, b_s, b_r, gg_s, gg_r,
    hb_s, hb_r, rb_s, rb_r, g2_s, g2_r, g3_s, g3_r, rs_s, rs_r,
):
    me = lax.axis_index("seq")
    z = me // N
    y = me % N
    total = N * N

    def dev(axis, off):
        if axis == "y":
            return z * N + (y + off + N) % N
        return ((z + off + N) % N) * N + y

    pos = {"y": y, "z": z}

    def rc(src, dst, ss, rs, to):
        return pltpu.make_async_remote_copy(
            src_ref=src, dst_ref=dst, send_sem=ss, recv_sem=rs, device_id={"seq": to}, device_id_type=MESH
        )

    locals_ = []
    for i in range(ITEMS):
        part_of = (pl.ds(i // HEADS * BLK, BLK), pl.ds(i % HEADS * HD, HD))
        locals_.append(pltpu.make_async_copy(k.at[part_of], agk.at[y, i], lsem.at[i]))
        locals_.append(pltpu.make_async_copy(v.at[part_of], agv.at[z, i], lsem.at[ITEMS + i]))
    win_own = [
        pltpu.make_async_copy(k, wink.at[pl.ds(BLK, 2 * BLK)], lsem.at[2 * ITEMS]),
        pltpu.make_async_copy(v, winv.at[pl.ds(BLK, 2 * BLK)], lsem.at[2 * ITEMS + 1]),
    ]
    list_copies = [
        pltpu.make_async_copy(lists, rbv, lsem.at[2 * ITEMS + 2]),
        pltpu.make_async_copy(lists, rbs, lsem.at[2 * ITEMS + 3]),
    ]
    query_copies = [
        pltpu.make_async_copy(q_hbm, q, lsem.at[2 * ITEMS + 4]),
        pltpu.make_async_copy(g_hbm, g, lsem.at[2 * ITEMS + 5]),
    ]
    for c in list_copies + locals_ + win_own + query_copies:
        c.start()

    barrier = pltpu.get_barrier_semaphore()
    right_seq = (me + 1) % total
    left_seq = (me + total - 1) % total

    def greet(d, carry):
        pl.semaphore_signal(barrier, inc=1, device_id={"seq": dev("y", d)}, device_id_type=MESH)
        pl.semaphore_signal(barrier, inc=1, device_id={"seq": dev("z", d)}, device_id_type=MESH)
        return carry

    lax.fori_loop(1, N, greet, 0)
    pl.semaphore_signal(barrier, inc=1, device_id={"seq": right_seq}, device_id_type=MESH)
    pl.semaphore_signal(barrier, inc=1, device_id={"seq": left_seq}, device_id_type=MESH)
    for c in list_copies:
        c.wait()
    src_ids = lax.broadcasted_iota(jnp.int32, (N * N, 2 * N * N), 0)
    parity = lax.broadcasted_iota(jnp.int32, (1, 2 * N * N), 1) % 2
    want = jnp.zeros((N * N, 2 * N * N), jnp.int32)
    for h in range(HEADS):
        for r in range(NRAND):
            row = rbv[r, pl.ds(h, 1), :]
            entry = row % 2 * HEADS + (h + 1 + 16 * (2 * (h * NRAND + r))) + 16 * parity
            want = jnp.maximum(want, jnp.where(row // 2 == src_ids, entry, 0))
    tvm[...] = want

    for c in locals_:
        c.wait()
    to_scalars = pltpu.make_async_copy(tvm, tsm, tsem)
    to_scalars.start()
    pl.semaphore_wait(barrier, 2 * N)

    def ag_copy(arr, i):
        dr, s, c = AG[i]
        axis, buf = (("y", agk), ("z", agv))[arr]
        slot = (pos[axis] - dr * (s - 1) + N) % N
        rows = pl.ds(c * HEADS, HEADS)
        return rc(buf.at[slot, rows], buf.at[slot, rows], ag_s.at[arr, i], ag_r.at[arr, i], dev(axis, dr))

    def ag_wait(arr, i):
        dr, s, c = AG[i]
        axis, buf = (("y", agk), ("z", agv))[arr]
        slot = (pos[axis] - dr * s + N) % N
        rows = pl.ds(c * HEADS, HEADS)
        rc(buf.at[slot, rows], buf.at[slot, rows], ag_s.at[arr, i], ag_r.at[arr, i], dev(axis, dr)).wait_recv()

    index = {key: i for i, key in enumerate(AG)}
    for i, (dr, s, c) in enumerate(AG):
        if s == 1:
            for arr in (0, 1):
                ag_copy(arr, i).start()

    halo = [
        rc(k.at[pl.ds(BLK, BLK)], wink.at[pl.ds(0, BLK)], h_s.at[0], h_r.at[0], right_seq),
        rc(v.at[pl.ds(BLK, BLK)], winv.at[pl.ds(0, BLK)], h_s.at[1], h_r.at[1], right_seq),
        rc(k.at[pl.ds(0, BLK)], wink.at[pl.ds(3 * BLK, BLK)], h_s.at[2], h_r.at[2], left_seq),
        rc(v.at[pl.ds(0, BLK)], winv.at[pl.ds(3 * BLK, BLK)], h_s.at[3], h_r.at[3], left_seq),
    ]

    for i, (dr, s, c) in enumerate(AG):
        for arr in (0, 1):
            ag_wait(arr, i)
            nxt = index.get((dr, s + 1, c))
            if nxt is not None:
                ag_copy(arr, nxt).start()
        if i == 3:
            for c_ in halo:
                c_.start()
    for c in win_own + query_copies:
        c.wait()
    to_scalars.wait()

    def entry_of(s, dest):
        return jnp.maximum(tsm[s, 2 * dest], tsm[s, 2 * dest + 1])

    def item(buf, slot, code):
        return buf[slot, code]

    gblk = [glb[i] for i in range(NGLOB)]

    def pick(idx):
        return jnp.where(idx // HEADS == 0, gblk[0], gblk[1])

    def far_first(j):
        return jnp.where(j % 2 == 1, N // 2 - (j + 1) // 2, N // 2 + j // 2)

    blk = pick(y)
    gsk[...] = item(agk, blk // 2 % N, blk % 2 * HEADS + y % HEADS)
    gck[z] = gsk[...]
    blk = pick(z)
    gsv[...] = item(agv, blk // (2 * N), blk % 2 * HEADS + z % HEADS)
    gcv[y] = gsv[...]

    def eighth(j, carry):
        d = far_first(j)
        rc(gsk, gck.at[z], gc_s.at[0, j], gc_r.at[0, j], dev("z", d)).start()
        rc(gsv, gcv.at[y], gc_s.at[1, j], gc_r.at[1, j], dev("y", d)).start()
        return carry

    lax.fori_loop(0, N - 1, eighth, 0)

    def code_of(s, dest):
        return jnp.maximum(entry_of(s, dest) % 16 - 1, 0)

    def fill(dst_k, dst_v, zd, yd):
        for s in range(N):
            dst_k[s] = item(agk, s, code_of(z * N + s, zd * N + y))
            dst_v[s] = item(agv, s, code_of(s * N + y, z * N + yd))

    def bundle(j, carry):
        d = far_first(j)
        zd = (z + d) % N
        yd = (y + d) % N
        fill(sk.at[j], sv.at[j], zd, yd)
        rc(sk.at[j], rk.at[z], b_s.at[0, j], b_r.at[0, j], zd * N + y).start()
        rc(sv.at[j], rv.at[y], b_s.at[1, j], b_r.at[1, j], z * N + yd).start()
        return carry

    lax.fori_loop(0, N - 1, bundle, 0)
    fill(rk.at[z], rv.at[y], z, y)

    def eighth_wait(j, carry):
        d = far_first(j)
        zs = (z + N - d) % N
        ys = (y + N - d) % N
        rc(gsk, gck.at[zs], gc_s.at[0, j], gc_r.at[0, j], zs * N + y).wait_recv()
        rc(gsv, gcv.at[ys], gc_s.at[1, j], gc_r.at[1, j], z * N + ys).wait_recv()
        return carry

    def small(src_k, src_v, ss, rs, axis_k, axis_v):
        def start(j, carry):
            d = j + 1
            rc(src_k.at[pos[axis_k]], src_k.at[pos[axis_k]], ss.at[0, j], rs.at[0, j], dev(axis_k, d)).start()
            rc(src_v.at[pos[axis_v]], src_v.at[pos[axis_v]], ss.at[1, j], rs.at[1, j], dev(axis_v, d)).start()
            return carry

        lax.fori_loop(0, N - 1, start, 0)

    def small_wait(src_k, src_v, ss, rs, axis_k, axis_v):
        def wait(j, carry):
            d = N - 1 - j
            sl = (pos[axis_k] + d) % N
            rc(src_k.at[sl], src_k.at[sl], ss.at[0, j], rs.at[0, j], dev(axis_k, d)).wait_recv()
            sl = (pos[axis_v] + d) % N
            rc(src_v.at[sl], src_v.at[sl], ss.at[1, j], rs.at[1, j], dev(axis_v, d)).wait_recv()
            return carry

        lax.fori_loop(0, N - 1, wait, 0)

    lax.fori_loop(0, N - 1, eighth_wait, 0)
    gk[y] = gck[pick(y) // (2 * N)]
    gv[z] = gcv[pick(z) // 2 % N]
    small(gk, gv, gg_s, gg_r, "y", "z")
    for c_ in halo:
        c_.wait_recv()

    def bundle_wait(j, carry):
        d = far_first(j)
        zs = (z + N - d) % N
        ys = (y + N - d) % N
        rc(sk.at[j], rk.at[zs], b_s.at[0, j], b_r.at[0, j], zs * N + y).wait_recv()
        rc(sv.at[j], rv.at[ys], b_s.at[1, j], b_r.at[1, j], z * N + ys).wait_recv()
        return carry

    lax.fori_loop(0, N - 1, bundle_wait, 0)
    small_wait(gk, gv, gg_s, gg_r, "y", "z")

    scale = HD ** (-0.5)
    key_count = (3 + NRAND + NGLOB) * BLK

    def head(h, carry):
        cols = pl.ds(pl.multiple_of(h * HD, HD), HD)
        for b in range(2):
            rows = pl.ds(b * BLK, BLK)
            kb, vb = ka.at[b], va.at[b]
            kb[pl.ds(0, 3 * BLK)] = wink[pl.ds(b * BLK, 3 * BLK), cols]
            vb[pl.ds(0, 3 * BLK)] = winv[pl.ds(b * BLK, 3 * BLK), cols]
            for r in range(NRAND):
                src = rbs[r, h, 2 * me + b] // 2
                kb[pl.ds((3 + r) * BLK, BLK)] = rk[src // N, src % N]
                vb[pl.ds((3 + r) * BLK, BLK)] = rv[src % N, src // N]
            for gi in range(NGLOB):
                kb[pl.ds((6 + gi) * BLK, BLK)] = gk[gi * HEADS + h]
                vb[pl.ds((6 + gi) * BLK, BLK)] = gv[gi * HEADS + h]
            kall, vall = kb[...], vb[...]
            qb, gb = q[rows, cols], g[rows, cols]
            s = lax.dot_general(qb, kall, ROWS_T, preferred_element_type=F32) * scale
            key_id = lax.broadcasted_iota(jnp.int32, (BLK, key_count), 1)
            if b == 0:
                bad = (key_id < BLK) & (me == 0)
            else:
                bad = (key_id >= 2 * BLK) & (key_id < 3 * BLK) & (me == total - 1)
            s = jnp.where(bad, -jnp.inf, s)
            m = jnp.max(s, -1, keepdims=True)
            e = jnp.exp(s - m)
            p = e * (1.0 / jnp.sum(e, -1, keepdims=True))
            plow = p.astype(BF16)
            o = lax.dot_general(plow, vall, (((1,), (0,)), ((), ())), preferred_element_type=F32).astype(BF16)
            delta = jnp.sum(gb.astype(F32) * o.astype(F32), -1, keepdims=True)
            dp = lax.dot_general(gb, vall, ROWS_T, preferred_element_type=F32)
            ds = (scale * p * (dp - delta)).astype(BF16)
            att[rows, cols] = o
            dq[rows, cols] = lax.dot_general(
                ds, kall, (((1,), (0,)), ((), ())), preferred_element_type=F32
            ).astype(BF16)
            for lhs, rhs, win, term, gacc in ((ds, qb, wk, termk, gak), (plow, gb, wv, termv, gav)):
                t = lax.dot_general(lhs, rhs, COLS_T, preferred_element_type=F32)
                if b == 0:
                    win[pl.ds(0, 3 * BLK), cols] = t[: 3 * BLK]
                else:
                    win[pl.ds(BLK, 2 * BLK), cols] += t[: 2 * BLK]
                    win[pl.ds(3 * BLK, BLK), cols] = t[2 * BLK : 3 * BLK]
                for r in range(NRAND):
                    term[(h * NRAND + r) * 2 + b] = t[(3 + r) * BLK : (4 + r) * BLK].astype(BF16)
                for gi in range(NGLOB):
                    piece = t[(6 + gi) * BLK : (7 + gi) * BLK]
                    if b == 0:
                        gacc[gi * HEADS + h] = piece
                    else:
                        gacc[gi * HEADS + h] += piece
        return carry

    lax.fori_loop(0, HEADS, head, 0)

    def fill_back(dst_k, dst_v, zd, yd):
        for s in range(N):
            dst_k[s] = termk[entry_of(zd * N + s, me) // 16]
            dst_v[s] = termv[entry_of(s * N + yd, me) // 16]
        dst_k[N] = gak[zd].astype(BF16)
        dst_v[N] = gav[yd].astype(BF16)

    hsk[0] = wk[pl.ds(0, BLK)].astype(BF16)
    hsk[1] = wk[pl.ds(3 * BLK, BLK)].astype(BF16)
    hsv[0] = wv[pl.ds(0, BLK)].astype(BF16)
    hsv[1] = wv[pl.ds(3 * BLK, BLK)].astype(BF16)

    def back(j, carry):
        d = far_first(j)
        zd = (z + d) % N
        yd = (y + d) % N
        fill_back(rsk.at[j], rsv.at[j], zd, yd)
        rc(rsk.at[j], rrk.at[z], rb_s.at[0, j], rb_r.at[0, j], zd * N + y).start()
        rc(rsv.at[j], rrv.at[y], rb_s.at[1, j], rb_r.at[1, j], z * N + yd).start()
        return carry

    lax.fori_loop(0, N - 1, back, 0)
    fill_back(rrk.at[z], rrv.at[y], z, y)
    halo_back = [
        rc(hsk.at[0], hrk.at[1], hb_s.at[0], hb_r.at[0], left_seq),
        rc(hsk.at[1], hrk.at[0], hb_s.at[1], hb_r.at[1], right_seq),
        rc(hsv.at[0], hrv.at[1], hb_s.at[2], hb_r.at[2], left_seq),
        rc(hsv.at[1], hrv.at[0], hb_s.at[3], hb_r.at[3], right_seq),
    ]
    for c_ in halo_back:
        c_.start()

    def back_wait(j, carry):
        d = far_first(j)
        zs = (z + N - d) % N
        ys = (y + N - d) % N
        rc(rsk.at[j], rrk.at[zs], rb_s.at[0, j], rb_r.at[0, j], zs * N + y).wait_recv()
        rc(rsv.at[j], rrv.at[ys], rb_s.at[1, j], rb_r.at[1, j], z * N + ys).wait_recv()
        return carry

    lax.fori_loop(0, N - 1, back_wait, 0)

    def total_of(read):
        acc = read(0).astype(F32)
        for s in range(1, N):
            acc += read(s).astype(F32)
        return acc.astype(BF16)

    g2k[y] = total_of(lambda s: rrk[s, N])
    g2v[z] = total_of(lambda s: rrv[s, N])
    small(g2k, g2v, g2_s, g2_r, "y", "z")

    tile = 16

    def partial(rel):
        for buf, part, p in ((rrk, pk, y), (rrv, pv, z)):
            tgt = (p + rel) % N
            weight = []
            for s in range(N):
                if buf is rrk:
                    code = entry_of(z * N + tgt, s * N + y) % 16
                else:
                    code = entry_of(tgt * N + y, z * N + s) % 16
                weight.append([jnp.where(code == i + 1, 1.0, 0.0).astype(F32) for i in range(ITEMS)])

            def rows_step(i, carry, buf=buf, part=part, tgt=tgt, weight=weight):
                rows = pl.ds(pl.multiple_of(i * tile, tile), tile)
                acc = [None] * ITEMS
                for s in range(N):
                    x = buf[s, tgt, rows].astype(F32)
                    for c in range(ITEMS):
                        w = x * weight[s][c]
                        acc[c] = w if acc[c] is None else acc[c] + w
                for c in range(ITEMS):
                    part[tgt, c, rows] = acc[c]
                return carry

            lax.fori_loop(0, BLK // tile, rows_step, 0)

    rs_index = {key: i for i, key in enumerate(RS)}

    def rs_copy(arr, i):
        f, s = RS[i]
        return rc(rsend.at[arr, i], rrecv.at[arr, i], rs_s.at[arr, i], rs_r.at[arr, i],
                  dev(("y", "z")[arr], FLOWS[f][0]))

    def rs_send(f, s):
        dr, c, hops = FLOWS[f]
        i = rs_index[(f, s)]
        for arr, part, p in ((0, pk, y), (1, pv, z)):
            tgt = (p + dr * (hops - s + 1) + N) % N
            x = part[tgt, pl.ds(c * HEADS, HEADS)]
            if s > 1:
                j = rs_index[(f, s - 1)]
                rs_copy(arr, j).wait_recv()
                x = x + rrecv[arr, j].astype(F32)
            rsend[arr, i] = x.astype(BF16)
            rs_copy(arr, i).start()

    def step_loop(first, stride, count):
        def body(j, carry):
            partial(first + stride * j)
            return carry

        lax.fori_loop(0, count, body, 0)

    step_loop(3, 1, 3)
    for f in range(4):
        rs_send(f, 1)
    step_loop(2, 4, 2)
    for f in range(4):
        rs_send(f, 2)
    small_wait(g2k, g2v, g2_s, g2_r, "y", "z")
    g3k[z] = total_of(lambda s: g2k[s])
    g3v[y] = total_of(lambda s: g2v[s])
    small(g3k, g3v, g3_s, g3_r, "z", "y")
    step_loop(0, 1, 2)
    step_loop(7, 1, 1)
    for f in range(4):
        rs_send(f, 3)
    for f in range(2):
        rs_send(f, 4)
    for c_ in halo_back:
        c_.wait_recv()
    small_wait(g3k, g3v, g3_s, g3_r, "z", "y")

    for f in (2, 3, 0, 1):
        for arr in (0, 1):
            rs_copy(arr, rs_index[(f, FLOWS[f][2])]).wait_recv()
    for arr, part, p, win, hr, g3, out in (
        (0, pk, y, wk, hrk, g3k, dk),
        (1, pv, z, wv, hrv, g3v, dv),
    ):
        for b in range(2):
            flows = [f for f in range(4) if FLOWS[f][1] == b]
            for h in range(HEADS):
                cols = pl.ds(h * HD, HD)
                x = win[pl.ds((1 + b) * BLK, BLK), cols] + hr[b, :, cols].astype(F32)
                x += part[p, b * HEADS + h]
                for f in flows:
                    x += rrecv[arr, rs_index[(f, FLOWS[f][2])], h].astype(F32)
                for gi in range(NGLOB):
                    mine = jnp.where(gblk[gi] == me * 2 + b, 1.0, 0.0).astype(F32)
                    x += g3[gi * HEADS + h].astype(F32) * mine
                out[pl.ds(b * BLK, BLK), cols] = x.astype(BF16)

    for arr in (0, 1):
        for i in range(len(AG)):
            ag_copy(arr, i).wait_send()
        for i in range(len(RS)):
            rs_copy(arr, i).wait_send()
    for c_ in halo + halo_back:
        c_.wait_send()

    def drain(j, carry):
        for a, (bk, bv) in ((b_s, (sk, sv)), (rb_s, (rsk, rsv))):
            rc(bk.at[j], rk.at[z], a.at[0, j], b_r.at[0, j], me).wait_send()
            rc(bv.at[j], rv.at[y], a.at[1, j], b_r.at[1, j], me).wait_send()
        for a, (bk, bv), (ik, iv) in (
            (gg_s, (gk, gv), (y, z)),
            (g2_s, (g2k, g2v), (y, z)),
            (g3_s, (g3k, g3v), (z, y)),
        ):
            rc(bk.at[ik], bk.at[ik], a.at[0, j], gg_r.at[0, j], me).wait_send()
            rc(bv.at[iv], bv.at[iv], a.at[1, j], gg_r.at[1, j], me).wait_send()
        rc(gsk, gck.at[z], gc_s.at[0, j], gc_r.at[0, j], me).wait_send()
        rc(gsv, gcv.at[y], gc_s.at[1, j], gc_r.at[1, j], me).wait_send()
        return carry

    lax.fori_loop(0, N - 1, drain, 0)


def settle(*refs):
    for src, dst in zip(refs[:4], refs[4:]):
        dst[...] = src[...]


def body(queries, keys, values, out_grad, random_blocks, global_blocks):
    lists = random_blocks.transpose(1, 0, 2)
    full = jax.ShapeDtypeStruct(queries.shape, BF16)
    vm, dma = pltpu.VMEM, pltpu.SemaphoreType.DMA
    bund = lambda n, slots: vm((n, slots, BLK, HD), BF16)
    keys_n = (3 + NRAND + NGLOB) * BLK
    small = vm((N, BLK, HD), BF16)
    scratch = [
        vm(queries.shape, BF16), vm(queries.shape, BF16),
        vm(lists.shape, jnp.int32), pltpu.SMEM(lists.shape, jnp.int32),
        vm((N * N, 2 * N * N), jnp.int32), pltpu.SMEM((N * N, 2 * N * N), jnp.int32),
        vm((BLK, HD), BF16), vm((BLK, HD), BF16), small, small,
        vm((N, ITEMS, BLK, HD), BF16), vm((N, ITEMS, BLK, HD), BF16),
        vm((4 * BLK, HEADS * HD), BF16), vm((4 * BLK, HEADS * HD), BF16),
        bund(N - 1, N), bund(N - 1, N), bund(N, N), bund(N, N),
        vm((N, BLK, HD), BF16), vm((N, BLK, HD), BF16),
        vm((2, keys_n, HD), BF16), vm((2, keys_n, HD), BF16),
        vm((24, BLK, HD), BF16), vm((24, BLK, HD), BF16),
        vm((4 * BLK, HEADS * HD), F32), vm((4 * BLK, HEADS * HD), F32),
        vm((N, BLK, HD), F32), vm((N, BLK, HD), F32),
        vm((2, BLK, HEADS * HD), BF16), vm((2, BLK, HEADS * HD), BF16),
        vm((2, BLK, HEADS * HD), BF16), vm((2, BLK, HEADS * HD), BF16),
        bund(N - 1, N + 1), bund(N - 1, N + 1), bund(N, N + 1), bund(N, N + 1),
        vm((N, ITEMS, BLK, HD), F32), vm((N, ITEMS, BLK, HD), F32),
        vm((N, BLK, HD), BF16), vm((N, BLK, HD), BF16),
        vm((N, BLK, HD), BF16), vm((N, BLK, HD), BF16),
        vm((2, len(RS), HEADS, BLK, HD), BF16), vm((2, len(RS), HEADS, BLK, HD), BF16),
        dma, dma((2, N - 1)), dma((2, N - 1)), dma((2 * ITEMS + 6,)), dma((2, len(AG))), dma((2, len(AG))), dma((4,)), dma((4,)),
        dma((2, N - 1)), dma((2, N - 1)), dma((2, N - 1)), dma((2, N - 1)),
        dma((4,)), dma((4,)), dma((2, N - 1)), dma((2, N - 1)),
        dma((2, N - 1)), dma((2, N - 1)), dma((2, N - 1)), dma((2, N - 1)),
        dma((2, len(RS))), dma((2, len(RS))),
    ]
    spec = pl.BlockSpec(memory_space=pltpu.VMEM)
    smem = pl.BlockSpec(memory_space=pltpu.SMEM)
    outs = pl.pallas_call(
        kernel,
        out_shape=(full,) * 4,
        in_specs=[smem] + [pl.BlockSpec(memory_space=pltpu.MemorySpace.HBM)] * 5,
        out_specs=(spec,) * 4,
        scratch_shapes=scratch,
        compiler_params=pltpu.CompilerParams(collective_id=0, has_side_effects=True),
    )(global_blocks, lists, queries, keys, values, out_grad)
    return pl.pallas_call(
        settle,
        out_shape=(full,) * 4,
        in_specs=[spec] * 4,
        out_specs=(spec,) * 4,
    )(*outs)


def solution(mesh):
    wide = P(("dp", "seq"), "heads")
    return jax.shard_map(
        body,
        mesh=mesh,
        in_specs=(wide, wide, wide, wide, P(("dp", "heads"), None, None), P("dp")),
        out_specs=(wide,) * 4,
        check_vma=False,
    )
```

```python
import jax
import jax.numpy as jnp
from jax import lax
from jax.experimental import pallas as pl
from jax.experimental.pallas import tpu as pltpu
from jax.sharding import PartitionSpec as P

MESH = pl.DeviceIdType.MESH
BLK = 64
HD = 128
N = 8
HEADS = 4
NRAND = 3
NGLOB = 2
ITEMS = 2 * HEADS
F32 = jnp.float32
BF16 = jnp.bfloat16
ROWS_T = (((1,), (1,)), ((), ()))
COLS_T = (((0,), (0,)), ((), ()))

AG = [(dr, s, c) for s in range(1, 5) for c in (0, 1) for dr in (1, -1) if s < 4 or (dr == 1) == (c == 0)]
FLOWS = [(1, 0, 4), (-1, 1, 4), (1, 1, 3), (-1, 0, 3)]
RS = [(f, s) for s in range(1, 5) for f in range(4) if s <= FLOWS[f][2]]


def kernel(
    glb, lists, q_hbm, k, v, g_hbm,
    att, dq, dk, dv,
    q, g, rbv, rbs,
    tvm, tsm, gsk, gsv, gck, gcv,
    agk, agv, winv, sk, sv, rk, rv, gk, gv,
    ka1, va1, ka2, va2, s1, dp1, p2, ds2, stat, rimk, rimt, gsbk, gsbv, grk, grv,
    termk, termv, wk, wv, gak, gav, hsk, hsv, hrv,
    rsk, rsv, rrk, rrv, pk, pv, g2k, g2v, g3k, g3v,
    rsend, rrecv,
    g1_s, g1_r, tsem, gc_s, gc_r, lsem, ag_s, ag_r, h_s, h_r, b_s, b_r, gg_s, gg_r,
    hb_s, hb_r, rb_s, rb_r, g2_s, g2_r, g3_s, g3_r, rs_s, rs_r,
):
    me = lax.axis_index("seq")
    z = me // N
    y = me % N
    total = N * N

    def dev(axis, off):
        if axis == "y":
            return z * N + (y + off + N) % N
        return ((z + off + N) % N) * N + y

    pos = {"y": y, "z": z}

    def rc(src, dst, ss, rs, to):
        return pltpu.make_async_remote_copy(
            src_ref=src, dst_ref=dst, send_sem=ss, recv_sem=rs, device_id={"seq": to}, device_id_type=MESH
        )

    locals_ = []
    for i in range(ITEMS):
        part_of = (pl.ds(i // HEADS * BLK, BLK), pl.ds(i % HEADS * HD, HD))
        locals_.append(pltpu.make_async_copy(k.at[part_of], agk.at[y, i], lsem.at[i]))
        locals_.append(pltpu.make_async_copy(v.at[part_of], agv.at[z, i], lsem.at[ITEMS + i]))
    win_own = [
        pltpu.make_async_copy(v, winv.at[pl.ds(BLK, 2 * BLK)], lsem.at[2 * ITEMS + 1]),
    ]
    list_copies = [
        pltpu.make_async_copy(lists, rbv, lsem.at[2 * ITEMS + 2]),
        pltpu.make_async_copy(lists, rbs, lsem.at[2 * ITEMS + 3]),
    ]
    query_copies = [
        pltpu.make_async_copy(q_hbm, q, lsem.at[2 * ITEMS + 4]),
        pltpu.make_async_copy(g_hbm, g, lsem.at[2 * ITEMS + 5]),
    ]
    for c in list_copies + locals_ + win_own + query_copies:
        c.start()

    barrier = pltpu.get_barrier_semaphore()
    right_seq = (me + 1) % total
    left_seq = (me + total - 1) % total

    def greet(d, carry):
        pl.semaphore_signal(barrier, inc=1, device_id={"seq": dev("y", d)}, device_id_type=MESH)
        pl.semaphore_signal(barrier, inc=1, device_id={"seq": dev("z", d)}, device_id_type=MESH)
        return carry

    lax.fori_loop(1, N, greet, 0)
    pl.semaphore_signal(barrier, inc=1, device_id={"seq": right_seq}, device_id_type=MESH)
    pl.semaphore_signal(barrier, inc=1, device_id={"seq": left_seq}, device_id_type=MESH)
    for c in list_copies:
        c.wait()
    src_ids = lax.broadcasted_iota(jnp.int32, (N * N, 2 * N * N), 0)
    parity = lax.broadcasted_iota(jnp.int32, (1, 2 * N * N), 1) % 2
    want = jnp.zeros((N * N, 2 * N * N), jnp.int32)
    for h in range(HEADS):
        for r in range(NRAND):
            row = rbv[r, pl.ds(h, 1), :]
            entry = row % 2 * HEADS + (h + 1 + 16 * (2 * (h * NRAND + r))) + 16 * parity
            want = jnp.maximum(want, jnp.where(row // 2 == src_ids, entry, 0))
    tvm[...] = want

    for c in locals_:
        c.wait()
    to_scalars = pltpu.make_async_copy(tvm, tsm, tsem)
    to_scalars.start()
    pl.semaphore_wait(barrier, 2 * N)

    def ag_copy(arr, i):
        dr, s, c = AG[i]
        axis, buf = (("y", agk), ("z", agv))[arr]
        slot = (pos[axis] - dr * (s - 1) + N) % N
        rows = pl.ds(c * HEADS, HEADS)
        return rc(buf.at[slot, rows], buf.at[slot, rows], ag_s.at[arr, i], ag_r.at[arr, i], dev(axis, dr))

    def ag_wait(arr, i):
        dr, s, c = AG[i]
        axis, buf = (("y", agk), ("z", agv))[arr]
        slot = (pos[axis] - dr * s + N) % N
        rows = pl.ds(c * HEADS, HEADS)
        rc(buf.at[slot, rows], buf.at[slot, rows], ag_s.at[arr, i], ag_r.at[arr, i], dev(axis, dr)).wait_recv()

    index = {key: i for i, key in enumerate(AG)}
    for i, (dr, s, c) in enumerate(AG):
        if s == 1:
            for arr in (0, 1):
                ag_copy(arr, i).start()

    halo = [
        rc(v.at[pl.ds(BLK, BLK)], winv.at[pl.ds(0, BLK)], h_s.at[1], h_r.at[1], right_seq),
        rc(v.at[pl.ds(0, BLK)], winv.at[pl.ds(3 * BLK, BLK)], h_s.at[3], h_r.at[3], left_seq),
    ]

    for i, (dr, s, c) in enumerate(AG):
        for arr in (0, 1):
            ag_wait(arr, i)
            nxt = index.get((dr, s + 1, c))
            if nxt is not None:
                ag_copy(arr, nxt).start()
        if i == 3:
            for c_ in halo:
                c_.start()
    for c in win_own + query_copies:
        c.wait()
    to_scalars.wait()

    def entry_of(s, dest):
        return jnp.maximum(tsm[s, 2 * dest], tsm[s, 2 * dest + 1])

    def item(buf, slot, code):
        return buf[slot, code]

    gblk = [glb[i] for i in range(NGLOB)]

    def pick(idx):
        return jnp.where(idx // HEADS == 0, gblk[0], gblk[1])

    def far_first(j):
        return jnp.where(j % 2 == 1, N // 2 - (j + 1) // 2, N // 2 + j // 2)

    blk = pick(y)
    gsk[...] = item(agk, blk // 2 % N, blk % 2 * HEADS + y % HEADS)
    gck[z] = gsk[...]
    blk = pick(z)
    gsv[...] = item(agv, blk // (2 * N), blk % 2 * HEADS + z % HEADS)
    gcv[y] = gsv[...]

    def eighth(j, carry):
        d = far_first(j)
        rc(gsk, gck.at[z], gc_s.at[0, j], gc_r.at[0, j], dev("z", d)).start()
        rc(gsv, gcv.at[y], gc_s.at[1, j], gc_r.at[1, j], dev("y", d)).start()
        return carry

    lax.fori_loop(0, N - 1, eighth, 0)

    key_rims = [
        (0, rc(agk.at[N - 1, pl.ds(HEADS, HEADS)], rimk.at[0], h_s.at[0], h_r.at[0], dev("z", 1))),
        (N - 1, rc(agk.at[0, pl.ds(0, HEADS)], rimk.at[1], h_s.at[2], h_r.at[2], dev("z", -1))),
    ]
    for end, copy in key_rims:
        pl.when(y == end)(copy.start)

    @pl.when(y > 0)
    def _():
        rimk[0] = agk[(y + N - 1) % N, pl.ds(HEADS, HEADS)]

    @pl.when(y < N - 1)
    def _():
        rimk[1] = agk[(y + 1) % N, pl.ds(0, HEADS)]


    def code_of(s, dest):
        return jnp.maximum(entry_of(s, dest) % 16 - 1, 0)

    def fill(dst_k, dst_v, zd, yd):
        for s in range(N):
            dst_k[s] = item(agk, s, code_of(z * N + s, zd * N + y))
            dst_v[s] = item(agv, s, code_of(s * N + y, z * N + yd))

    def bundle(j, carry):
        d = far_first(j)
        zd = (z + d) % N
        yd = (y + d) % N
        fill(sk.at[j], sv.at[j], zd, yd)
        rc(sk.at[j], rk.at[z], b_s.at[0, j], b_r.at[0, j], zd * N + y).start()
        rc(sv.at[j], rv.at[y], b_s.at[1, j], b_r.at[1, j], z * N + yd).start()
        return carry

    early = 3
    lax.fori_loop(0, early, bundle, 0)

    def eighth_wait(j, carry):
        d = far_first(j)
        zs = (z + N - d) % N
        ys = (y + N - d) % N
        rc(gsk, gck.at[zs], gc_s.at[0, j], gc_r.at[0, j], zs * N + y).wait_recv()
        rc(gsv, gcv.at[ys], gc_s.at[1, j], gc_r.at[1, j], z * N + ys).wait_recv()
        return carry

    def small(src_k, src_v, ss, rs, axis_k, axis_v):
        def start(j, carry):
            d = j + 1
            rc(src_k.at[pos[axis_k]], src_k.at[pos[axis_k]], ss.at[0, j], rs.at[0, j], dev(axis_k, d)).start()
            rc(src_v.at[pos[axis_v]], src_v.at[pos[axis_v]], ss.at[1, j], rs.at[1, j], dev(axis_v, d)).start()
            return carry

        lax.fori_loop(0, N - 1, start, 0)

    def small_wait(src_k, src_v, ss, rs, axis_k, axis_v):
        def wait(j, carry):
            d = N - 1 - j
            sl = (pos[axis_k] + d) % N
            rc(src_k.at[sl], src_k.at[sl], ss.at[0, j], rs.at[0, j], dev(axis_k, d)).wait_recv()
            sl = (pos[axis_v] + d) % N
            rc(src_v.at[sl], src_v.at[sl], ss.at[1, j], rs.at[1, j], dev(axis_v, d)).wait_recv()
            return carry

        lax.fori_loop(0, N - 1, wait, 0)

    lax.fori_loop(0, N - 1, eighth_wait, 0)
    gk[y] = gck[pick(y) // (2 * N)]
    gv[z] = gcv[pick(z) // 2 % N]
    small(gk, gv, gg_s, gg_r, "y", "z")
    lax.fori_loop(early, N - 1, bundle, 0)
    fill(rk.at[z], rv.at[y], z, y)
    for c_ in halo:
        c_.wait_recv()
    for end, copy in key_rims:
        pl.when(y == end)(copy.wait_recv)
    small_wait(gk, gv, gg_s, gg_r, "y", "z")

    def bundle_wait(j, carry):
        d = far_first(j)
        zs = (z + N - d) % N
        ys = (y + N - d) % N
        rc(sk.at[j], rk.at[zs], b_s.at[0, j], b_r.at[0, j], zs * N + y).wait_recv()
        rc(sv.at[j], rv.at[ys], b_s.at[1, j], b_r.at[1, j], z * N + ys).wait_recv()
        return carry

    scale = HD ** (-0.5)
    near = (3 + NGLOB) * BLK
    rows_by_cols = (((1,), (0,)), ((), ()))

    def dot(lhs, rhs, dims):
        return lax.dot_general(lhs, rhs, dims, preferred_element_type=F32)

    def over_pairs(one):
        def head(h, carry):
            cols = pl.ds(pl.multiple_of(h * HD, HD), HD)
            for b in range(2):
                one(h, b, 2 * h + b, pl.ds(b * BLK, BLK), cols)
            return carry

        lax.fori_loop(0, HEADS, head, 0)

    def first(h, b, i, rows, cols):
        trio = (rimk[0, h], agk[y, h], agk[y, HEADS + h], rimk[1, h])
        for j in range(3):
            ka1[i, pl.ds(j * BLK, BLK)] = trio[b + j]
        va1[i, pl.ds(0, 3 * BLK)] = winv[pl.ds(b * BLK, 3 * BLK), cols]
        for buf, glo in ((ka1, gk), (va1, gv)):
            for gi in range(NGLOB):
                buf[i, pl.ds((3 + gi) * BLK, BLK)] = glo[gi * HEADS + h]
        s = dot(q[rows, cols], ka1[i], ROWS_T) * scale
        key_id = lax.broadcasted_iota(jnp.int32, (BLK, near), 1)
        if b == 0:
            bad = (key_id < BLK) & (me == 0)
        else:
            bad = (key_id >= 2 * BLK) & (key_id < 3 * BLK) & (me == total - 1)
        s = jnp.where(bad, -jnp.inf, s)
        m = jnp.max(s, -1, keepdims=True)
        e = jnp.exp(s - m)
        dp = dot(g[rows, cols], va1[i], ROWS_T)
        s1[i], dp1[i] = e, dp
        stat[0, i] = m
        stat[1, i] = jnp.sum(e, -1, keepdims=True)
        stat[2, i] = jnp.sum(e * dp, -1, keepdims=True)

    over_pairs(first)
    lax.fori_loop(0, N - 1, bundle_wait, 0)

    def second(h, b, i, rows, cols):
        for r in range(NRAND):
            src = rbs[r, h, 2 * me + b] // 2
            ka2[i, pl.ds(r * BLK, BLK)] = rk[src // N, src % N]
            va2[i, pl.ds(r * BLK, BLK)] = rv[src % N, src // N]
        qb, gb = q[rows, cols], g[rows, cols]
        far = dot(qb, ka2[i], ROWS_T) * scale
        dp2 = dot(gb, va2[i], ROWS_T)
        m1 = stat[0, i]
        m = jnp.maximum(m1, jnp.max(far, -1, keepdims=True))
        shrink = jnp.exp(m1 - m)
        ef = jnp.exp(far - m)
        inv = 1.0 / (shrink * stat[1, i] + jnp.sum(ef, -1, keepdims=True))
        delta = (shrink * stat[2, i] + jnp.sum(ef * dp2, -1, keepdims=True)) * inv
        pf = ef * inv
        pf_low = pf.astype(BF16)
        dsf = (scale * pf * (dp2 - delta)).astype(BF16)
        p2[i], ds2[i] = pf_low, dsf
        stat[0, i] = shrink * inv
        stat[1, i] = delta
        for lhs, rhs, term in ((dsf, qb, termk), (pf_low, gb, termv)):
            t = dot(lhs, rhs, COLS_T)
            for r in range(NRAND):
                term[(h * NRAND + r) * 2 + b] = t[r * BLK : (r + 1) * BLK].astype(BF16)

    for h in range(HEADS):
        for b in range(2):
            second(h, b, 2 * h + b, pl.ds(b * BLK, BLK), pl.ds(h * HD, HD))

    def fill_back(dst_k, dst_v, zd, yd):
        for s in range(N):
            dst_k[s] = termk[entry_of(zd * N + s, me) // 16]
            dst_v[s] = termv[entry_of(s * N + yd, me) // 16]

    def back(j, carry):
        d = far_first(j)
        zd = (z + d) % N
        yd = (y + d) % N
        fill_back(rsk.at[j], rsv.at[j], zd, yd)
        rc(rsk.at[j], rrk.at[z], rb_s.at[0, j], rb_r.at[0, j], zd * N + y).start()
        rc(rsv.at[j], rrv.at[y], rb_s.at[1, j], rb_r.at[1, j], z * N + yd).start()
        return carry

    lax.fori_loop(0, N - 1, back, 0)
    fill_back(rrk.at[z], rrv.at[y], z, y)

    def third(h, b, i, rows, cols):
        qb, gb = q[rows, cols], g[rows, cols]
        pn = s1[i] * stat[0, i]
        pn_low = pn.astype(BF16)
        dsn = (scale * pn * (dp1[i] - stat[1, i])).astype(BF16)
        att[rows, cols] = (dot(pn_low, va1[i], rows_by_cols) + dot(p2[i], va2[i], rows_by_cols)).astype(BF16)
        dq[rows, cols] = (dot(dsn, ka1[i], rows_by_cols) + dot(ds2[i], ka2[i], rows_by_cols)).astype(BF16)
        for lhs, rhs, win, gacc in ((dsn, qb, wk, gak), (pn_low, gb, wv, gav)):
            t = dot(lhs, rhs, COLS_T)
            if b == 0:
                win[pl.ds(0, 3 * BLK), cols] = t[: 3 * BLK]
            else:
                win[pl.ds(BLK, 2 * BLK), cols] += t[: 2 * BLK]
                win[pl.ds(3 * BLK, BLK), cols] = t[2 * BLK : 3 * BLK]
            for gi in range(NGLOB):
                piece = t[(3 + gi) * BLK : (4 + gi) * BLK]
                if b == 0:
                    gacc[gi * HEADS + h] = piece
                else:
                    gacc[gi * HEADS + h] += piece

    over_pairs(third)
    for h in range(HEADS):
        hsk[0, h] = wk[pl.ds(0, BLK), pl.ds(h * HD, HD)].astype(BF16)
        hsk[1, h] = wk[pl.ds(3 * BLK, BLK), pl.ds(h * HD, HD)].astype(BF16)
    hsv[0] = wv[pl.ds(0, BLK)].astype(BF16)
    hsv[1] = wv[pl.ds(3 * BLK, BLK)].astype(BF16)
    gsbk[...] = gak[...].astype(BF16)
    gsbv[...] = gav[...].astype(BF16)
    grk[z] = gak[z].astype(BF16)
    grv[y] = gav[y].astype(BF16)

    def glob_back(j, carry):
        d = far_first(j)
        zd = (z + d) % N
        yd = (y + d) % N
        rc(gsbk.at[zd], grk.at[z], g1_s.at[0, j], g1_r.at[0, j], zd * N + y).start()
        rc(gsbv.at[yd], grv.at[y], g1_s.at[1, j], g1_r.at[1, j], z * N + yd).start()
        return carry

    def glob_back_wait(j, carry):
        d = far_first(j)
        zs = (z + N - d) % N
        ys = (y + N - d) % N
        rc(gsbk.at[zs], grk.at[zs], g1_s.at[0, j], g1_r.at[0, j], zs * N + y).wait_recv()
        rc(gsbv.at[ys], grv.at[ys], g1_s.at[1, j], g1_r.at[1, j], z * N + ys).wait_recv()
        return carry

    lax.fori_loop(0, N - 1, glob_back, 0)
    halo_back = [
        rc(hsv.at[0], hrv.at[1], hb_s.at[2], hb_r.at[2], left_seq),
        rc(hsv.at[1], hrv.at[0], hb_s.at[3], hb_r.at[3], right_seq),
    ]
    rim_back = [
        (0, rc(hsk.at[0], rimt.at[0], hb_s.at[0], hb_r.at[0], dev("z", -1))),
        (N - 1, rc(hsk.at[1], rimt.at[1], hb_s.at[1], hb_r.at[1], dev("z", 1))),
    ]
    for end, copy in rim_back:
        pl.when(y == end)(copy.start)
    for c_ in halo_back:
        c_.start()

    def back_wait(j, carry):
        d = far_first(j)
        zs = (z + N - d) % N
        ys = (y + N - d) % N
        rc(rsk.at[j], rrk.at[zs], rb_s.at[0, j], rb_r.at[0, j], zs * N + y).wait_recv()
        rc(rsv.at[j], rrv.at[ys], rb_s.at[1, j], rb_r.at[1, j], z * N + ys).wait_recv()
        return carry

    tile = 16
    arrivals = [(0, 4, 3, 5), (2, 6), (1, 7)]

    def partial(rel, wave):
        for buf, part, p in ((rrk, pk, y), (rrv, pv, z)):
            tgt = (p + rel) % N
            weight, rows_of = [], []
            for d in arrivals[wave]:
                if buf is rrk:
                    s = (z + N - d) % N
                    code = entry_of(z * N + tgt, s * N + y) % 16
                else:
                    s = (y + N - d) % N
                    code = entry_of(tgt * N + y, z * N + s) % 16
                rows_of.append(s)
                weight.append([jnp.where(code == i + 1, 1.0, 0.0).astype(F32) for i in range(ITEMS)])

            def rows_step(i, carry, buf=buf, part=part, tgt=tgt, weight=weight, rows_of=rows_of):
                rows = pl.ds(pl.multiple_of(i * tile, tile), tile)
                acc = [None if wave == 0 else part[tgt, c, rows] for c in range(ITEMS)]
                for s, ws in zip(rows_of, weight):
                    x = buf[s, tgt, rows].astype(F32)
                    for c in range(ITEMS):
                        w = x * ws[c]
                        acc[c] = w if acc[c] is None else acc[c] + w
                for c in range(ITEMS):
                    part[tgt, c, rows] = acc[c]
                return carry

            lax.fori_loop(0, BLK // tile, rows_step, 0)

    def step_loop(first_rel, stride, count, wave=2):
        def more(j, carry):
            partial((first_rel + stride * j) % N, wave)
            return carry

        lax.fori_loop(0, count, more, 0)

    lax.fori_loop(0, 3, back_wait, 0)
    step_loop(0, 1, N, 0)
    lax.fori_loop(3, 5, back_wait, 0)
    step_loop(0, 1, N, 1)
    for end, copy in rim_back:
        pl.when(y == end)(copy.wait_recv)

    @pl.when(y > 0)
    def _():
        pk[(y + N - 1) % N, pl.ds(HEADS, HEADS)] += hsk[0].astype(F32)

    @pl.when(y == 0)
    def _():
        pk[N - 1, pl.ds(HEADS, HEADS)] += rimt[0].astype(F32)

    @pl.when(y < N - 1)
    def _():
        pk[(y + 1) % N, pl.ds(0, HEADS)] += hsk[1].astype(F32)

    @pl.when(y == N - 1)
    def _():
        pk[0, pl.ds(0, HEADS)] += rimt[1].astype(F32)

    lax.fori_loop(5, N - 1, back_wait, 0)

    def total_of(read):
        acc = read(0).astype(F32)
        for s in range(1, N):
            acc += read(s).astype(F32)
        return acc.astype(BF16)

    rs_index = {key: i for i, key in enumerate(RS)}

    def rs_copy(arr, i):
        f, s = RS[i]
        return rc(rsend.at[arr, i], rrecv.at[arr, i], rs_s.at[arr, i], rs_r.at[arr, i],
                  dev(("y", "z")[arr], FLOWS[f][0]))

    def rs_send(f, s):
        dr, c, hops = FLOWS[f]
        i = rs_index[(f, s)]
        for arr, part, p in ((0, pk, y), (1, pv, z)):
            tgt = (p + dr * (hops - s + 1) + N) % N
            x = part[tgt, pl.ds(c * HEADS, HEADS)]
            if s > 1:
                j = rs_index[(f, s - 1)]
                rs_copy(arr, j).wait_recv()
                x = x + rrecv[arr, j].astype(F32)
            rsend[arr, i] = x.astype(BF16)
            rs_copy(arr, i).start()

    step_loop(3, 1, 3)
    for f in range(4):
        rs_send(f, 1)
    step_loop(2, 4, 2)
    lax.fori_loop(0, N - 1, glob_back_wait, 0)
    g2k[y] = total_of(lambda s: grk[s])
    g2v[z] = total_of(lambda s: grv[s])
    small(g2k, g2v, g2_s, g2_r, "y", "z")
    for f in range(4):
        rs_send(f, 2)
    step_loop(7, 1, 3)
    small_wait(g2k, g2v, g2_s, g2_r, "y", "z")
    g3k[z] = total_of(lambda s: g2k[s])
    g3v[y] = total_of(lambda s: g2v[s])
    small(g3k, g3v, g3_s, g3_r, "z", "y")
    for f in range(4):
        rs_send(f, 3)
    for f in range(2):
        rs_send(f, 4)
    for c_ in halo_back:
        c_.wait_recv()
    small_wait(g3k, g3v, g3_s, g3_r, "z", "y")

    parts = ((0, pk, y, wk, None, g3k, dk), (1, pv, z, wv, hrv, g3v, dv))
    for arr, part, p, win, hr, g3, out in parts:
        for b in range(2):
            mine = [jnp.where(gblk[gi] == me * 2 + b, 1.0, 0.0).astype(F32) for gi in range(NGLOB)]
            for h in range(HEADS):
                cols = pl.ds(h * HD, HD)
                x = part[p, b * HEADS + h] + win[pl.ds((1 + b) * BLK, BLK), cols]
                if hr is not None:
                    x += hr[b, :, cols].astype(F32)
                for gi in range(NGLOB):
                    x += g3[gi * HEADS + h].astype(F32) * mine[gi]
                part[p, b * HEADS + h] = x
    for f in (2, 3, 0, 1):
        i = rs_index[(f, FLOWS[f][2])]
        b = FLOWS[f][1]
        for arr, part, p, win, hr, g3, out in parts:
            rs_copy(arr, i).wait_recv()
            for h in range(HEADS):
                x = part[p, b * HEADS + h] + rrecv[arr, i, h].astype(F32)
                if f < 2:
                    out[pl.ds(b * BLK, BLK), pl.ds(h * HD, HD)] = x.astype(BF16)
                else:
                    part[p, b * HEADS + h] = x

    for arr in (0, 1):
        for i in range(len(AG)):
            ag_copy(arr, i).wait_send()
        for i in range(len(RS)):
            rs_copy(arr, i).wait_send()
    for c_ in halo + halo_back:
        c_.wait_send()
    for end, copy in key_rims + rim_back:
        pl.when(y == end)(copy.wait_send)

    def drain(j, carry):
        for a, (bk, bv) in ((b_s, (sk, sv)), (rb_s, (rsk, rsv))):
            rc(bk.at[j], rk.at[z], a.at[0, j], b_r.at[0, j], me).wait_send()
            rc(bv.at[j], rv.at[y], a.at[1, j], b_r.at[1, j], me).wait_send()
        for a, (bk, bv), (ik, iv) in (
            (gg_s, (gk, gv), (y, z)),
            (g2_s, (g2k, g2v), (y, z)),
            (g3_s, (g3k, g3v), (z, y)),
        ):
            rc(bk.at[ik], bk.at[ik], a.at[0, j], gg_r.at[0, j], me).wait_send()
            rc(bv.at[iv], bv.at[iv], a.at[1, j], gg_r.at[1, j], me).wait_send()
        rc(gsbk.at[z], grk.at[z], g1_s.at[0, j], g1_r.at[0, j], me).wait_send()
        rc(gsbv.at[y], grv.at[y], g1_s.at[1, j], g1_r.at[1, j], me).wait_send()
        rc(gsk, gck.at[z], gc_s.at[0, j], gc_r.at[0, j], me).wait_send()
        rc(gsv, gcv.at[y], gc_s.at[1, j], gc_r.at[1, j], me).wait_send()
        return carry

    lax.fori_loop(0, N - 1, drain, 0)


def settle(*refs):
    for src, dst in zip(refs[:4], refs[4:]):
        dst[...] = src[...]


def body(queries, keys, values, out_grad, random_blocks, global_blocks):
    lists = random_blocks.transpose(1, 0, 2)
    full = jax.ShapeDtypeStruct(queries.shape, BF16)
    vm, dma = pltpu.VMEM, pltpu.SemaphoreType.DMA
    bund = lambda n, slots: vm((n, slots, BLK, HD), BF16)
    near, far = (3 + NGLOB) * BLK, NRAND * BLK
    small = vm((N, BLK, HD), BF16)
    scratch = [
        vm(queries.shape, BF16), vm(queries.shape, BF16),
        vm(lists.shape, jnp.int32), pltpu.SMEM(lists.shape, jnp.int32),
        vm((N * N, 2 * N * N), jnp.int32), pltpu.SMEM((N * N, 2 * N * N), jnp.int32),
        vm((BLK, HD), BF16), vm((BLK, HD), BF16), small, small,
        vm((N, ITEMS, BLK, HD), BF16), vm((N, ITEMS, BLK, HD), BF16),
        vm((4 * BLK, HEADS * HD), BF16),
        bund(N - 1, N), bund(N - 1, N), bund(N, N), bund(N, N),
        vm((N, BLK, HD), BF16), vm((N, BLK, HD), BF16),
        vm((ITEMS, near, HD), BF16), vm((ITEMS, near, HD), BF16),
        vm((ITEMS, far, HD), BF16), vm((ITEMS, far, HD), BF16),
        vm((ITEMS, BLK, near), F32), vm((ITEMS, BLK, near), F32),
        vm((ITEMS, BLK, far), BF16), vm((ITEMS, BLK, far), BF16),
        vm((3, ITEMS, BLK, 1), F32), vm((2, HEADS, BLK, HD), BF16), vm((2, HEADS, BLK, HD), BF16),
        small, small, small, small,
        vm((24, BLK, HD), BF16), vm((24, BLK, HD), BF16),
        vm((4 * BLK, HEADS * HD), F32), vm((4 * BLK, HEADS * HD), F32),
        vm((N, BLK, HD), F32), vm((N, BLK, HD), F32),
        vm((2, HEADS, BLK, HD), BF16), vm((2, BLK, HEADS * HD), BF16),
        vm((2, BLK, HEADS * HD), BF16),
        bund(N - 1, N), bund(N - 1, N), bund(N, N), bund(N, N),
        vm((N, ITEMS, BLK, HD), F32), vm((N, ITEMS, BLK, HD), F32),
        vm((N, BLK, HD), BF16), vm((N, BLK, HD), BF16),
        vm((N, BLK, HD), BF16), vm((N, BLK, HD), BF16),
        vm((2, len(RS), HEADS, BLK, HD), BF16), vm((2, len(RS), HEADS, BLK, HD), BF16),
        dma((2, N - 1)), dma((2, N - 1)),
        dma, dma((2, N - 1)), dma((2, N - 1)), dma((2 * ITEMS + 6,)), dma((2, len(AG))), dma((2, len(AG))), dma((4,)), dma((4,)),
        dma((2, N - 1)), dma((2, N - 1)), dma((2, N - 1)), dma((2, N - 1)),
        dma((4,)), dma((4,)), dma((2, N - 1)), dma((2, N - 1)),
        dma((2, N - 1)), dma((2, N - 1)), dma((2, N - 1)), dma((2, N - 1)),
        dma((2, len(RS))), dma((2, len(RS))),
    ]
    spec = pl.BlockSpec(memory_space=pltpu.VMEM)
    smem = pl.BlockSpec(memory_space=pltpu.SMEM)
    outs = pl.pallas_call(
        kernel,
        out_shape=(full,) * 4,
        in_specs=[smem] + [pl.BlockSpec(memory_space=pltpu.MemorySpace.HBM)] * 5,
        out_specs=(spec,) * 4,
        scratch_shapes=scratch,
        compiler_params=pltpu.CompilerParams(collective_id=0, has_side_effects=True),
    )(global_blocks, lists, queries, keys, values, out_grad)
    return pl.pallas_call(
        settle,
        out_shape=(full,) * 4,
        in_specs=[spec] * 4,
        out_specs=(spec,) * 4,
    )(*outs)


def solution(mesh):
    wide = P(("dp", "seq"), "heads")
    return jax.shard_map(
        body,
        mesh=mesh,
        in_specs=(wide, wide, wide, wide, P(("dp", "heads"), None, None), P("dp")),
        out_specs=(wide,) * 4,
        check_vma=False,
    )
```

```python
import jax
import jax.numpy as jnp
from jax import lax
from jax.experimental import pallas as pl
from jax.experimental.pallas import tpu as pltpu
from jax.sharding import PartitionSpec as P

MESH = pl.DeviceIdType.MESH
BLK = 64
HD = 128
N = 8
HEADS = 4
NRAND = 3
NGLOB = 2
ITEMS = 2 * HEADS
F32 = jnp.float32
BF16 = jnp.bfloat16
ROWS_T = (((1,), (1,)), ((), ()))
COLS_T = (((0,), (0,)), ((), ()))

AG = [(dr, s, c) for s in range(1, 5) for c in (0, 1) for dr in (1, -1) if s < 4 or (dr == 1) == (c == 0)]
FLOWS = [(1, 0, 4), (-1, 1, 4), (1, 1, 3), (-1, 0, 3)]
RS = [(f, s) for s in range(1, 5) for f in range(4) if s <= FLOWS[f][2]]


def kernel(
    glb, lists, q_hbm, k, v, g_hbm,
    att, dq, dk, dv,
    q, g, rbv, rbs,
    tvm, tsm, gsk, gsv, gck, gcv,
    agk, agv, winv, sk, sv, rk, rv, gk, gv,
    ka1, va1, ka2, va2, s1, dp1, p2, ds2, stat, rimk, rimt, gsbk, gsbv, grk, grv,
    termk, termv, wk, wv, gak, gav, hsk, hsv, hrv,
    rsk, rsv, rrk, rrv, pk, pv, g2k, g2v, g3k, g3v,
    rsend, rrecv,
    g1_s, g1_r, tsem, gc_s, gc_r, lsem, ag_s, ag_r, h_s, h_r, b_s, b_r, gg_s, gg_r,
    hb_s, hb_r, rb_s, rb_r, g2_s, g2_r, g3_s, g3_r, rs_s, rs_r,
):
    me = lax.axis_index("seq")
    z = me // N
    y = me % N
    total = N * N

    def dev(axis, off):
        if axis == "y":
            return z * N + (y + off + N) % N
        return ((z + off + N) % N) * N + y

    pos = {"y": y, "z": z}

    def rc(src, dst, ss, rs, to):
        return pltpu.make_async_remote_copy(
            src_ref=src, dst_ref=dst, send_sem=ss, recv_sem=rs, device_id={"seq": to}, device_id_type=MESH
        )

    locals_ = []
    for i in range(ITEMS):
        part_of = (pl.ds(i // HEADS * BLK, BLK), pl.ds(i % HEADS * HD, HD))
        locals_.append(pltpu.make_async_copy(k.at[part_of], agk.at[y, i], lsem.at[i]))
        locals_.append(pltpu.make_async_copy(v.at[part_of], agv.at[z, i], lsem.at[ITEMS + i]))
    win_own = [
        pltpu.make_async_copy(v, winv.at[pl.ds(BLK, 2 * BLK)], lsem.at[2 * ITEMS + 1]),
    ]
    list_copies = [
        pltpu.make_async_copy(lists, rbv, lsem.at[2 * ITEMS + 2]),
        pltpu.make_async_copy(lists, rbs, lsem.at[2 * ITEMS + 3]),
    ]
    query_copies = [
        pltpu.make_async_copy(q_hbm, q, lsem.at[2 * ITEMS + 4]),
        pltpu.make_async_copy(g_hbm, g, lsem.at[2 * ITEMS + 5]),
    ]
    for c in list_copies + locals_ + win_own + query_copies:
        c.start()

    barrier = pltpu.get_barrier_semaphore()
    right_seq = (me + 1) % total
    left_seq = (me + total - 1) % total

    def greet(d, carry):
        pl.semaphore_signal(barrier, inc=1, device_id={"seq": dev("y", d)}, device_id_type=MESH)
        pl.semaphore_signal(barrier, inc=1, device_id={"seq": dev("z", d)}, device_id_type=MESH)
        return carry

    lax.fori_loop(1, N, greet, 0)
    pl.semaphore_signal(barrier, inc=1, device_id={"seq": right_seq}, device_id_type=MESH)
    pl.semaphore_signal(barrier, inc=1, device_id={"seq": left_seq}, device_id_type=MESH)
    for c in list_copies:
        c.wait()
    src_ids = lax.broadcasted_iota(jnp.int32, (N * N, 2 * N * N), 0)
    parity = lax.broadcasted_iota(jnp.int32, (1, 2 * N * N), 1) % 2
    want = jnp.zeros((N * N, 2 * N * N), jnp.int32)
    for h in range(HEADS):
        for r in range(NRAND):
            row = rbv[r, pl.ds(h, 1), :]
            entry = row % 2 * HEADS + (h + 1 + 16 * (2 * (h * NRAND + r))) + 16 * parity
            want = jnp.maximum(want, jnp.where(row // 2 == src_ids, entry, 0))
    tvm[...] = want

    for c in locals_:
        c.wait()
    to_scalars = pltpu.make_async_copy(tvm, tsm, tsem)
    to_scalars.start()
    pl.semaphore_wait(barrier, 2 * N)

    def ag_copy(arr, i):
        dr, s, c = AG[i]
        axis, buf = (("y", agk), ("z", agv))[arr]
        slot = (pos[axis] - dr * (s - 1) + N) % N
        rows = pl.ds(c * HEADS, HEADS)
        return rc(buf.at[slot, rows], buf.at[slot, rows], ag_s.at[arr, i], ag_r.at[arr, i], dev(axis, dr))

    def ag_wait(arr, i):
        dr, s, c = AG[i]
        axis, buf = (("y", agk), ("z", agv))[arr]
        slot = (pos[axis] - dr * s + N) % N
        rows = pl.ds(c * HEADS, HEADS)
        rc(buf.at[slot, rows], buf.at[slot, rows], ag_s.at[arr, i], ag_r.at[arr, i], dev(axis, dr)).wait_recv()

    index = {key: i for i, key in enumerate(AG)}
    for i, (dr, s, c) in enumerate(AG):
        if s == 1:
            for arr in (0, 1):
                ag_copy(arr, i).start()

    halo = [
        rc(v.at[pl.ds(BLK, BLK)], winv.at[pl.ds(0, BLK)], h_s.at[1], h_r.at[1], right_seq),
        rc(v.at[pl.ds(0, BLK)], winv.at[pl.ds(3 * BLK, BLK)], h_s.at[3], h_r.at[3], left_seq),
    ]

    for i, (dr, s, c) in enumerate(AG):
        for arr in (0, 1):
            ag_wait(arr, i)
            nxt = index.get((dr, s + 1, c))
            if nxt is not None:
                ag_copy(arr, nxt).start()
        if i == 3:
            for c_ in halo:
                c_.start()
    for c in win_own + query_copies:
        c.wait()
    to_scalars.wait()

    def entry_of(s, dest):
        return jnp.maximum(tsm[s, 2 * dest], tsm[s, 2 * dest + 1])

    def item(buf, slot, code):
        return buf[slot, code]

    gblk = [glb[i] for i in range(NGLOB)]

    def pick(idx):
        return jnp.where(idx // HEADS == 0, gblk[0], gblk[1])

    def far_first(j):
        return jnp.where(j % 2 == 1, N // 2 - (j + 1) // 2, N // 2 + j // 2)

    blk = pick(y)
    gsk[...] = item(agk, blk // 2 % N, blk % 2 * HEADS + y % HEADS)
    gck[z] = gsk[...]
    blk = pick(z)
    gsv[...] = item(agv, blk // (2 * N), blk % 2 * HEADS + z % HEADS)
    gcv[y] = gsv[...]

    def eighth(j, carry):
        d = far_first(j)
        rc(gsk, gck.at[z], gc_s.at[0, j], gc_r.at[0, j], dev("z", d)).start()
        rc(gsv, gcv.at[y], gc_s.at[1, j], gc_r.at[1, j], dev("y", d)).start()
        return carry

    lax.fori_loop(0, N - 1, eighth, 0)

    key_rims = [
        (0, rc(agk.at[N - 1, pl.ds(HEADS, HEADS)], rimk.at[0], h_s.at[0], h_r.at[0], dev("z", 1))),
        (N - 1, rc(agk.at[0, pl.ds(0, HEADS)], rimk.at[1], h_s.at[2], h_r.at[2], dev("z", -1))),
    ]
    for end, copy in key_rims:
        pl.when(y == end)(copy.start)

    @pl.when(y > 0)
    def _():
        rimk[0] = agk[(y + N - 1) % N, pl.ds(HEADS, HEADS)]

    @pl.when(y < N - 1)
    def _():
        rimk[1] = agk[(y + 1) % N, pl.ds(0, HEADS)]


    def code_of(s, dest):
        return jnp.maximum(entry_of(s, dest) % 16 - 1, 0)

    def fill(dst_k, dst_v, zd, yd):
        for s in range(N):
            dst_k[s] = item(agk, s, code_of(z * N + s, zd * N + y))
            dst_v[s] = item(agv, s, code_of(s * N + y, z * N + yd))

    def bundle(j, carry):
        d = far_first(j)
        zd = (z + d) % N
        yd = (y + d) % N
        fill(sk.at[j], sv.at[j], zd, yd)
        rc(sk.at[j], rk.at[z], b_s.at[0, j], b_r.at[0, j], zd * N + y).start()
        rc(sv.at[j], rv.at[y], b_s.at[1, j], b_r.at[1, j], z * N + yd).start()
        return carry

    early = 3
    lax.fori_loop(0, early, bundle, 0)

    def eighth_wait(j, carry):
        d = far_first(j)
        zs = (z + N - d) % N
        ys = (y + N - d) % N
        rc(gsk, gck.at[zs], gc_s.at[0, j], gc_r.at[0, j], zs * N + y).wait_recv()
        rc(gsv, gcv.at[ys], gc_s.at[1, j], gc_r.at[1, j], z * N + ys).wait_recv()
        return carry

    def small(src_k, src_v, ss, rs, axis_k, axis_v):
        def start(j, carry):
            d = j + 1
            rc(src_k.at[pos[axis_k]], src_k.at[pos[axis_k]], ss.at[0, j], rs.at[0, j], dev(axis_k, d)).start()
            rc(src_v.at[pos[axis_v]], src_v.at[pos[axis_v]], ss.at[1, j], rs.at[1, j], dev(axis_v, d)).start()
            return carry

        lax.fori_loop(0, N - 1, start, 0)

    def small_wait(src_k, src_v, ss, rs, axis_k, axis_v):
        def wait(j, carry):
            d = N - 1 - j
            sl = (pos[axis_k] + d) % N
            rc(src_k.at[sl], src_k.at[sl], ss.at[0, j], rs.at[0, j], dev(axis_k, d)).wait_recv()
            sl = (pos[axis_v] + d) % N
            rc(src_v.at[sl], src_v.at[sl], ss.at[1, j], rs.at[1, j], dev(axis_v, d)).wait_recv()
            return carry

        lax.fori_loop(0, N - 1, wait, 0)

    lax.fori_loop(0, N - 1, eighth_wait, 0)
    gk[y] = gck[pick(y) // (2 * N)]
    gv[z] = gcv[pick(z) // 2 % N]
    small(gk, gv, gg_s, gg_r, "y", "z")
    lax.fori_loop(early, N - 1, bundle, 0)
    fill(rk.at[z], rv.at[y], z, y)
    for c_ in halo:
        c_.wait_recv()
    for end, copy in key_rims:
        pl.when(y == end)(copy.wait_recv)
    small_wait(gk, gv, gg_s, gg_r, "y", "z")

    def bundle_wait(j, carry):
        d = far_first(j)
        zs = (z + N - d) % N
        ys = (y + N - d) % N
        rc(sk.at[j], rk.at[zs], b_s.at[0, j], b_r.at[0, j], zs * N + y).wait_recv()
        rc(sv.at[j], rv.at[ys], b_s.at[1, j], b_r.at[1, j], z * N + ys).wait_recv()
        return carry

    scale = HD ** (-0.5)
    near = (3 + NGLOB) * BLK
    rows_by_cols = (((1,), (0,)), ((), ()))

    def dot(lhs, rhs, dims):
        return lax.dot_general(lhs, rhs, dims, preferred_element_type=F32)

    def over_pairs(one):
        def head(h, carry):
            cols = pl.ds(pl.multiple_of(h * HD, HD), HD)
            for b in range(2):
                one(h, b, 2 * h + b, pl.ds(b * BLK, BLK), cols)
            return carry

        lax.fori_loop(0, HEADS, head, 0)

    def first(h, b, i, rows, cols):
        trio = (rimk[0, h], agk[y, h], agk[y, HEADS + h], rimk[1, h])
        for j in range(3):
            ka1[i, pl.ds(j * BLK, BLK)] = trio[b + j]
        va1[i, pl.ds(0, 3 * BLK)] = winv[pl.ds(b * BLK, 3 * BLK), cols]
        for buf, glo in ((ka1, gk), (va1, gv)):
            for gi in range(NGLOB):
                buf[i, pl.ds((3 + gi) * BLK, BLK)] = glo[gi * HEADS + h]
        s = dot(q[rows, cols], ka1[i], ROWS_T) * scale
        key_id = lax.broadcasted_iota(jnp.int32, (BLK, near), 1)
        if b == 0:
            bad = (key_id < BLK) & (me == 0)
        else:
            bad = (key_id >= 2 * BLK) & (key_id < 3 * BLK) & (me == total - 1)
        s = jnp.where(bad, -jnp.inf, s)
        m = jnp.max(s, -1, keepdims=True)
        e = jnp.exp(s - m)
        dp = dot(g[rows, cols], va1[i], ROWS_T)
        s1[i], dp1[i] = e, dp
        stat[0, i] = m
        stat[1, i] = jnp.sum(e, -1, keepdims=True)
        stat[2, i] = jnp.sum(e * dp, -1, keepdims=True)

    over_pairs(first)
    lax.fori_loop(0, N - 1, bundle_wait, 0)

    def second(h, b, i, rows, cols):
        for r in range(NRAND):
            src = rbs[r, h, 2 * me + b] // 2
            ka2[i, pl.ds(r * BLK, BLK)] = rk[src // N, src % N]
            va2[i, pl.ds(r * BLK, BLK)] = rv[src % N, src // N]
        qb, gb = q[rows, cols], g[rows, cols]
        far = dot(qb, ka2[i], ROWS_T) * scale
        dp2 = dot(gb, va2[i], ROWS_T)
        m1 = stat[0, i]
        m = jnp.maximum(m1, jnp.max(far, -1, keepdims=True))
        shrink = jnp.exp(m1 - m)
        ef = jnp.exp(far - m)
        inv = 1.0 / (shrink * stat[1, i] + jnp.sum(ef, -1, keepdims=True))
        delta = (shrink * stat[2, i] + jnp.sum(ef * dp2, -1, keepdims=True)) * inv
        pf = ef * inv
        pf_low = pf.astype(BF16)
        dsf = (scale * pf * (dp2 - delta)).astype(BF16)
        p2[i], ds2[i] = pf_low, dsf
        stat[0, i] = shrink * inv
        stat[1, i] = delta
        for lhs, rhs, term in ((dsf, qb, termk), (pf_low, gb, termv)):
            t = dot(lhs, rhs, COLS_T)
            for r in range(NRAND):
                term[(h * NRAND + r) * 2 + b] = t[r * BLK : (r + 1) * BLK].astype(BF16)

    for h in range(HEADS):
        for b in range(2):
            second(h, b, 2 * h + b, pl.ds(b * BLK, BLK), pl.ds(h * HD, HD))

    def fill_back(dst_k, dst_v, zd, yd):
        for s in range(N):
            dst_k[s] = termk[entry_of(zd * N + s, me) // 16]
            dst_v[s] = termv[entry_of(s * N + yd, me) // 16]

    def back(j, carry):
        d = far_first(j)
        zd = (z + d) % N
        yd = (y + d) % N
        fill_back(rsk.at[j], rsv.at[j], zd, yd)
        rc(rsk.at[j], rrk.at[z], rb_s.at[0, j], rb_r.at[0, j], zd * N + y).start()
        rc(rsv.at[j], rrv.at[y], rb_s.at[1, j], rb_r.at[1, j], z * N + yd).start()
        return carry

    lax.fori_loop(0, N - 1, back, 0)
    fill_back(rrk.at[z], rrv.at[y], z, y)

    def third(h, b, i, rows, cols):
        qb, gb = q[rows, cols], g[rows, cols]
        pn = s1[i] * stat[0, i]
        pn_low = pn.astype(BF16)
        dsn = (scale * pn * (dp1[i] - stat[1, i])).astype(BF16)
        att[rows, cols] = (dot(pn_low, va1[i], rows_by_cols) + dot(p2[i], va2[i], rows_by_cols)).astype(BF16)
        dq[rows, cols] = (dot(dsn, ka1[i], rows_by_cols) + dot(ds2[i], ka2[i], rows_by_cols)).astype(BF16)
        for lhs, rhs, win, gacc in ((dsn, qb, wk, gak), (pn_low, gb, wv, gav)):
            t = dot(lhs, rhs, COLS_T)
            if b == 0:
                win[pl.ds(0, 3 * BLK), cols] = t[: 3 * BLK]
            else:
                win[pl.ds(BLK, 2 * BLK), cols] += t[: 2 * BLK]
                win[pl.ds(3 * BLK, BLK), cols] = t[2 * BLK : 3 * BLK]
            for gi in range(NGLOB):
                piece = t[(3 + gi) * BLK : (4 + gi) * BLK]
                if b == 0:
                    gacc[gi * HEADS + h] = piece
                else:
                    gacc[gi * HEADS + h] += piece

    over_pairs(third)
    for h in range(HEADS):
        hsk[0, h] = wk[pl.ds(0, BLK), pl.ds(h * HD, HD)].astype(BF16)
        hsk[1, h] = wk[pl.ds(3 * BLK, BLK), pl.ds(h * HD, HD)].astype(BF16)
    hsv[0] = wv[pl.ds(0, BLK)].astype(BF16)
    hsv[1] = wv[pl.ds(3 * BLK, BLK)].astype(BF16)
    gsbk[...] = gak[...].astype(BF16)
    gsbv[...] = gav[...].astype(BF16)
    grk[z] = gak[z].astype(BF16)
    grv[y] = gav[y].astype(BF16)

    def glob_back(j, carry):
        d = far_first(j)
        zd = (z + d) % N
        yd = (y + d) % N
        rc(gsbk.at[zd], grk.at[z], g1_s.at[0, j], g1_r.at[0, j], zd * N + y).start()
        rc(gsbv.at[yd], grv.at[y], g1_s.at[1, j], g1_r.at[1, j], z * N + yd).start()
        return carry

    def glob_back_wait(j, carry):
        d = far_first(j)
        zs = (z + N - d) % N
        ys = (y + N - d) % N
        rc(gsbk.at[zs], grk.at[zs], g1_s.at[0, j], g1_r.at[0, j], zs * N + y).wait_recv()
        rc(gsbv.at[ys], grv.at[ys], g1_s.at[1, j], g1_r.at[1, j], z * N + ys).wait_recv()
        return carry

    lax.fori_loop(0, N - 1, glob_back, 0)
    halo_back = [
        rc(hsv.at[0], hrv.at[1], hb_s.at[2], hb_r.at[2], left_seq),
        rc(hsv.at[1], hrv.at[0], hb_s.at[3], hb_r.at[3], right_seq),
    ]
    rim_back = [
        (0, rc(hsk.at[0], rimt.at[0], hb_s.at[0], hb_r.at[0], dev("z", -1))),
        (N - 1, rc(hsk.at[1], rimt.at[1], hb_s.at[1], hb_r.at[1], dev("z", 1))),
    ]
    for end, copy in rim_back:
        pl.when(y == end)(copy.start)
    for c_ in halo_back:
        c_.start()

    def back_wait(j, carry):
        d = far_first(j)
        zs = (z + N - d) % N
        ys = (y + N - d) % N
        rc(rsk.at[j], rrk.at[zs], rb_s.at[0, j], rb_r.at[0, j], zs * N + y).wait_recv()
        rc(rsv.at[j], rrv.at[ys], rb_s.at[1, j], rb_r.at[1, j], z * N + ys).wait_recv()
        return carry

    tile = 16
    arrivals = [(0, 4, 3, 5), (2, 6), (1, 7)]

    def partial(rel, wave):
        for buf, part, p in ((rrk, pk, y), (rrv, pv, z)):
            tgt = (p + rel) % N
            weight, rows_of = [], []
            for d in arrivals[wave]:
                if buf is rrk:
                    s = (z + N - d) % N
                    code = entry_of(z * N + tgt, s * N + y) % 16
                else:
                    s = (y + N - d) % N
                    code = entry_of(tgt * N + y, z * N + s) % 16
                rows_of.append(s)
                weight.append([jnp.where(code == i + 1, 1.0, 0.0).astype(F32) for i in range(ITEMS)])

            def rows_step(i, carry, buf=buf, part=part, tgt=tgt, weight=weight, rows_of=rows_of):
                rows = pl.ds(pl.multiple_of(i * tile, tile), tile)
                acc = [None if wave == 0 else part[tgt, c, rows] for c in range(ITEMS)]
                for s, ws in zip(rows_of, weight):
                    x = buf[s, tgt, rows].astype(F32)
                    for c in range(ITEMS):
                        w = x * ws[c]
                        acc[c] = w if acc[c] is None else acc[c] + w
                for c in range(ITEMS):
                    part[tgt, c, rows] = acc[c]
                return carry

            lax.fori_loop(0, BLK // tile, rows_step, 0)

    def step_loop(first_rel, stride, count, wave=2):
        def more(j, carry):
            partial((first_rel + stride * j) % N, wave)
            return carry

        lax.fori_loop(0, count, more, 0)

    lax.fori_loop(0, 3, back_wait, 0)
    step_loop(0, 1, N, 0)
    lax.fori_loop(3, 5, back_wait, 0)
    step_loop(0, 1, N, 1)
    for end, copy in rim_back:
        pl.when(y == end)(copy.wait_recv)

    @pl.when(y > 0)
    def _():
        pk[(y + N - 1) % N, pl.ds(HEADS, HEADS)] += hsk[0].astype(F32)

    @pl.when(y == 0)
    def _():
        pk[N - 1, pl.ds(HEADS, HEADS)] += rimt[0].astype(F32)

    @pl.when(y < N - 1)
    def _():
        pk[(y + 1) % N, pl.ds(0, HEADS)] += hsk[1].astype(F32)

    @pl.when(y == N - 1)
    def _():
        pk[0, pl.ds(0, HEADS)] += rimt[1].astype(F32)

    lax.fori_loop(5, N - 1, back_wait, 0)

    def total_of(read):
        acc = read(0).astype(F32)
        for s in range(1, N):
            acc += read(s).astype(F32)
        return acc.astype(BF16)

    rs_index = {key: i for i, key in enumerate(RS)}

    def rs_copy(arr, i):
        f, s = RS[i]
        return rc(rsend.at[arr, i], rrecv.at[arr, i], rs_s.at[arr, i], rs_r.at[arr, i],
                  dev(("y", "z")[arr], FLOWS[f][0]))

    def rs_send(f, s):
        dr, c, hops = FLOWS[f]
        i = rs_index[(f, s)]
        for arr, part, p in ((0, pk, y), (1, pv, z)):
            tgt = (p + dr * (hops - s + 1) + N) % N
            x = part[tgt, pl.ds(c * HEADS, HEADS)]
            if s > 1:
                j = rs_index[(f, s - 1)]
                rs_copy(arr, j).wait_recv()
                x = x + rrecv[arr, j].astype(F32)
            rsend[arr, i] = x.astype(BF16)
            rs_copy(arr, i).start()

    step_loop(3, 1, 3)
    for f in range(4):
        rs_send(f, 1)
    step_loop(2, 4, 2)
    for f in range(4):
        rs_send(f, 2)
    lax.fori_loop(0, N - 1, glob_back_wait, 0)
    g2k[y] = total_of(lambda s: grk[s])
    g2v[z] = total_of(lambda s: grv[s])
    small(g2k, g2v, g2_s, g2_r, "y", "z")
    step_loop(7, 1, 3)
    for f in range(4):
        rs_send(f, 3)
    small_wait(g2k, g2v, g2_s, g2_r, "y", "z")
    g3k[z] = total_of(lambda s: g2k[s])
    g3v[y] = total_of(lambda s: g2v[s])
    small(g3k, g3v, g3_s, g3_r, "z", "y")
    for f in range(2):
        rs_send(f, 4)
    for c_ in halo_back:
        c_.wait_recv()
    small_wait(g3k, g3v, g3_s, g3_r, "z", "y")

    parts = ((0, pk, y, wk, None, g3k, dk), (1, pv, z, wv, hrv, g3v, dv))
    for arr, part, p, win, hr, g3, out in parts:
        for b in range(2):
            mine = [jnp.where(gblk[gi] == me * 2 + b, 1.0, 0.0).astype(F32) for gi in range(NGLOB)]
            for h in range(HEADS):
                cols = pl.ds(h * HD, HD)
                x = part[p, b * HEADS + h] + win[pl.ds((1 + b) * BLK, BLK), cols]
                if hr is not None:
                    x += hr[b, :, cols].astype(F32)
                for gi in range(NGLOB):
                    x += g3[gi * HEADS + h].astype(F32) * mine[gi]
                part[p, b * HEADS + h] = x
    for f in (2, 3, 0, 1):
        i = rs_index[(f, FLOWS[f][2])]
        b = FLOWS[f][1]
        for arr, part, p, win, hr, g3, out in parts:
            rs_copy(arr, i).wait_recv()
            for h in range(HEADS):
                x = part[p, b * HEADS + h] + rrecv[arr, i, h].astype(F32)
                if f < 2:
                    out[pl.ds(b * BLK, BLK), pl.ds(h * HD, HD)] = x.astype(BF16)
                else:
                    part[p, b * HEADS + h] = x

    for arr in (0, 1):
        for i in range(len(AG)):
            ag_copy(arr, i).wait_send()
        for i in range(len(RS)):
            rs_copy(arr, i).wait_send()
    for c_ in halo + halo_back:
        c_.wait_send()
    for end, copy in key_rims + rim_back:
        pl.when(y == end)(copy.wait_send)

    def drain(j, carry):
        for a, (bk, bv) in ((b_s, (sk, sv)), (rb_s, (rsk, rsv))):
            rc(bk.at[j], rk.at[z], a.at[0, j], b_r.at[0, j], me).wait_send()
            rc(bv.at[j], rv.at[y], a.at[1, j], b_r.at[1, j], me).wait_send()
        for a, (bk, bv), (ik, iv) in (
            (gg_s, (gk, gv), (y, z)),
            (g2_s, (g2k, g2v), (y, z)),
            (g3_s, (g3k, g3v), (z, y)),
        ):
            rc(bk.at[ik], bk.at[ik], a.at[0, j], gg_r.at[0, j], me).wait_send()
            rc(bv.at[iv], bv.at[iv], a.at[1, j], gg_r.at[1, j], me).wait_send()
        rc(gsbk.at[z], grk.at[z], g1_s.at[0, j], g1_r.at[0, j], me).wait_send()
        rc(gsbv.at[y], grv.at[y], g1_s.at[1, j], g1_r.at[1, j], me).wait_send()
        rc(gsk, gck.at[z], gc_s.at[0, j], gc_r.at[0, j], me).wait_send()
        rc(gsv, gcv.at[y], gc_s.at[1, j], gc_r.at[1, j], me).wait_send()
        return carry

    lax.fori_loop(0, N - 1, drain, 0)


def settle(*refs):
    for src, dst in zip(refs[:4], refs[4:]):
        dst[...] = src[...]


def body(queries, keys, values, out_grad, random_blocks, global_blocks):
    lists = random_blocks.transpose(1, 0, 2)
    full = jax.ShapeDtypeStruct(queries.shape, BF16)
    vm, dma = pltpu.VMEM, pltpu.SemaphoreType.DMA
    bund = lambda n, slots: vm((n, slots, BLK, HD), BF16)
    near, far = (3 + NGLOB) * BLK, NRAND * BLK
    small = vm((N, BLK, HD), BF16)
    scratch = [
        vm(queries.shape, BF16), vm(queries.shape, BF16),
        vm(lists.shape, jnp.int32), pltpu.SMEM(lists.shape, jnp.int32),
        vm((N * N, 2 * N * N), jnp.int32), pltpu.SMEM((N * N, 2 * N * N), jnp.int32),
        vm((BLK, HD), BF16), vm((BLK, HD), BF16), small, small,
        vm((N, ITEMS, BLK, HD), BF16), vm((N, ITEMS, BLK, HD), BF16),
        vm((4 * BLK, HEADS * HD), BF16),
        bund(N - 1, N), bund(N - 1, N), bund(N, N), bund(N, N),
        vm((N, BLK, HD), BF16), vm((N, BLK, HD), BF16),
        vm((ITEMS, near, HD), BF16), vm((ITEMS, near, HD), BF16),
        vm((ITEMS, far, HD), BF16), vm((ITEMS, far, HD), BF16),
        vm((ITEMS, BLK, near), F32), vm((ITEMS, BLK, near), F32),
        vm((ITEMS, BLK, far), BF16), vm((ITEMS, BLK, far), BF16),
        vm((3, ITEMS, BLK, 1), F32), vm((2, HEADS, BLK, HD), BF16), vm((2, HEADS, BLK, HD), BF16),
        small, small, small, small,
        vm((24, BLK, HD), BF16), vm((24, BLK, HD), BF16),
        vm((4 * BLK, HEADS * HD), F32), vm((4 * BLK, HEADS * HD), F32),
        vm((N, BLK, HD), F32), vm((N, BLK, HD), F32),
        vm((2, HEADS, BLK, HD), BF16), vm((2, BLK, HEADS * HD), BF16),
        vm((2, BLK, HEADS * HD), BF16),
        bund(N - 1, N), bund(N - 1, N), bund(N, N), bund(N, N),
        vm((N, ITEMS, BLK, HD), F32), vm((N, ITEMS, BLK, HD), F32),
        vm((N, BLK, HD), BF16), vm((N, BLK, HD), BF16),
        vm((N, BLK, HD), BF16), vm((N, BLK, HD), BF16),
        vm((2, len(RS), HEADS, BLK, HD), BF16), vm((2, len(RS), HEADS, BLK, HD), BF16),
        dma((2, N - 1)), dma((2, N - 1)),
        dma, dma((2, N - 1)), dma((2, N - 1)), dma((2 * ITEMS + 6,)), dma((2, len(AG))), dma((2, len(AG))), dma((4,)), dma((4,)),
        dma((2, N - 1)), dma((2, N - 1)), dma((2, N - 1)), dma((2, N - 1)),
        dma((4,)), dma((4,)), dma((2, N - 1)), dma((2, N - 1)),
        dma((2, N - 1)), dma((2, N - 1)), dma((2, N - 1)), dma((2, N - 1)),
        dma((2, len(RS))), dma((2, len(RS))),
    ]
    spec = pl.BlockSpec(memory_space=pltpu.VMEM)
    smem = pl.BlockSpec(memory_space=pltpu.SMEM)
    outs = pl.pallas_call(
        kernel,
        out_shape=(full,) * 4,
        in_specs=[smem] + [pl.BlockSpec(memory_space=pltpu.MemorySpace.HBM)] * 5,
        out_specs=(spec,) * 4,
        scratch_shapes=scratch,
        compiler_params=pltpu.CompilerParams(collective_id=0, has_side_effects=True),
    )(global_blocks, lists, queries, keys, values, out_grad)
    return pl.pallas_call(
        settle,
        out_shape=(full,) * 4,
        in_specs=[spec] * 4,
        out_specs=(spec,) * 4,
    )(*outs)


def solution(mesh):
    wide = P(("dp", "seq"), "heads")
    return jax.shard_map(
        body,
        mesh=mesh,
        in_specs=(wide, wide, wide, wide, P(("dp", "heads"), None, None), P("dp")),
        out_specs=(wide,) * 4,
        check_vma=False,
    )
```

```python
import jax
import jax.numpy as jnp
from jax import lax
from jax.experimental import pallas as pl
from jax.experimental.pallas import tpu as pltpu
from jax.sharding import PartitionSpec as P

MESH = pl.DeviceIdType.MESH
BLK = 64
HD = 128
N = 8
HEADS = 4
NRAND = 3
NGLOB = 2
ITEMS = 2 * HEADS
F32 = jnp.float32
BF16 = jnp.bfloat16
ROWS_T = (((1,), (1,)), ((), ()))
COLS_T = (((0,), (0,)), ((), ()))

AG = [(dr, s, c) for s in range(1, 5) for c in (0, 1) for dr in (1, -1) if s < 4 or (dr == 1) == (c == 0)]
FLOWS = [(1, 0, 4), (-1, 1, 4), (1, 1, 3), (-1, 0, 3)]
RS = [(f, s) for s in range(1, 5) for f in range(4) if s <= FLOWS[f][2]]


def kernel(
    glb, lists, q_hbm, k, v, g_hbm,
    att, dq, dk, dv,
    q, g, rbv, rbs,
    tvm, tsm, gsk, gsv, gck, gcv,
    agk, agv, winv, sk, sv, rk, rv, gk, gv,
    ka1, va1, ka2, va2, s1, dp1, p2, ds2, stat, rimk, rimt, gsbk, gsbv, grk, grv,
    termk, termv, wk, wv, gak, gav, hsk, hsv, hrv,
    rsk, rsv, rrk, rrv, pk, pv, g2k, g2v, g3k, g3v,
    rsend, rrecv,
    g1_s, g1_r, tsem, gc_s, gc_r, lsem, ag_s, ag_r, h_s, h_r, b_s, b_r, gg_s, gg_r,
    hb_s, hb_r, rb_s, rb_r, g2_s, g2_r, g3_s, g3_r, rs_s, rs_r,
):
    me = lax.axis_index("seq")
    z = me // N
    y = me % N
    total = N * N

    def dev(axis, off):
        if axis == "y":
            return z * N + (y + off + N) % N
        return ((z + off + N) % N) * N + y

    pos = {"y": y, "z": z}

    def rc(src, dst, ss, rs, to):
        return pltpu.make_async_remote_copy(
            src_ref=src, dst_ref=dst, send_sem=ss, recv_sem=rs, device_id={"seq": to}, device_id_type=MESH
        )

    locals_ = []
    for i in range(ITEMS):
        part_of = (pl.ds(i // HEADS * BLK, BLK), pl.ds(i % HEADS * HD, HD))
        locals_.append(pltpu.make_async_copy(k.at[part_of], agk.at[y, i], lsem.at[i]))
        locals_.append(pltpu.make_async_copy(v.at[part_of], agv.at[z, i], lsem.at[ITEMS + i]))
    win_own = [
        pltpu.make_async_copy(v, winv.at[pl.ds(BLK, 2 * BLK)], lsem.at[2 * ITEMS + 1]),
    ]
    list_copies = [
        pltpu.make_async_copy(lists, rbv, lsem.at[2 * ITEMS + 2]),
        pltpu.make_async_copy(lists, rbs, lsem.at[2 * ITEMS + 3]),
    ]
    query_copies = [
        pltpu.make_async_copy(q_hbm, q, lsem.at[2 * ITEMS + 4]),
        pltpu.make_async_copy(g_hbm, g, lsem.at[2 * ITEMS + 5]),
    ]
    for c in list_copies + locals_ + win_own + query_copies:
        c.start()

    barrier = pltpu.get_barrier_semaphore()
    right_seq = (me + 1) % total
    left_seq = (me + total - 1) % total

    def greet(d, carry):
        pl.semaphore_signal(barrier, inc=1, device_id={"seq": dev("y", d)}, device_id_type=MESH)
        pl.semaphore_signal(barrier, inc=1, device_id={"seq": dev("z", d)}, device_id_type=MESH)
        return carry

    lax.fori_loop(1, N, greet, 0)
    pl.semaphore_signal(barrier, inc=1, device_id={"seq": right_seq}, device_id_type=MESH)
    pl.semaphore_signal(barrier, inc=1, device_id={"seq": left_seq}, device_id_type=MESH)
    for c in list_copies:
        c.wait()
    src_ids = lax.broadcasted_iota(jnp.int32, (N * N, 2 * N * N), 0)
    parity = lax.broadcasted_iota(jnp.int32, (1, 2 * N * N), 1) % 2
    want = jnp.zeros((N * N, 2 * N * N), jnp.int32)
    for h in range(HEADS):
        for r in range(NRAND):
            row = rbv[r, pl.ds(h, 1), :]
            entry = row % 2 * HEADS + (h + 1 + 16 * (2 * (h * NRAND + r))) + 16 * parity
            want = jnp.maximum(want, jnp.where(row // 2 == src_ids, entry, 0))
    tvm[...] = want

    for c in locals_:
        c.wait()
    to_scalars = pltpu.make_async_copy(tvm, tsm, tsem)
    to_scalars.start()
    pl.semaphore_wait(barrier, 2 * N)

    def ag_copy(arr, i):
        dr, s, c = AG[i]
        axis, buf = (("y", agk), ("z", agv))[arr]
        slot = (pos[axis] - dr * (s - 1) + N) % N
        rows = pl.ds(c * HEADS, HEADS)
        return rc(buf.at[slot, rows], buf.at[slot, rows], ag_s.at[arr, i], ag_r.at[arr, i], dev(axis, dr))

    def ag_wait(arr, i):
        dr, s, c = AG[i]
        axis, buf = (("y", agk), ("z", agv))[arr]
        slot = (pos[axis] - dr * s + N) % N
        rows = pl.ds(c * HEADS, HEADS)
        rc(buf.at[slot, rows], buf.at[slot, rows], ag_s.at[arr, i], ag_r.at[arr, i], dev(axis, dr)).wait_recv()

    index = {key: i for i, key in enumerate(AG)}
    for i, (dr, s, c) in enumerate(AG):
        if s == 1:
            for arr in (0, 1):
                ag_copy(arr, i).start()

    halo = [
        rc(v.at[pl.ds(BLK, BLK)], winv.at[pl.ds(0, BLK)], h_s.at[1], h_r.at[1], right_seq),
        rc(v.at[pl.ds(0, BLK)], winv.at[pl.ds(3 * BLK, BLK)], h_s.at[3], h_r.at[3], left_seq),
    ]

    for i, (dr, s, c) in enumerate(AG):
        for arr in (0, 1):
            ag_wait(arr, i)
            nxt = index.get((dr, s + 1, c))
            if nxt is not None:
                ag_copy(arr, nxt).start()
        if i == 3:
            for c_ in halo:
                c_.start()
    for c in win_own + query_copies:
        c.wait()
    to_scalars.wait()

    def entry_of(s, dest):
        return jnp.maximum(tsm[s, 2 * dest], tsm[s, 2 * dest + 1])

    def item(buf, slot, code):
        return buf[slot, code]

    gblk = [glb[i] for i in range(NGLOB)]

    def pick(idx):
        return jnp.where(idx // HEADS == 0, gblk[0], gblk[1])

    def far_first(j):
        return jnp.where(j % 2 == 1, N // 2 - (j + 1) // 2, N // 2 + j // 2)

    blk = pick(y)
    gsk[...] = item(agk, blk // 2 % N, blk % 2 * HEADS + y % HEADS)
    gck[z] = gsk[...]
    blk = pick(z)
    gsv[...] = item(agv, blk // (2 * N), blk % 2 * HEADS + z % HEADS)
    gcv[y] = gsv[...]

    def eighth(j, carry):
        d = far_first(j)
        rc(gsk, gck.at[z], gc_s.at[0, j], gc_r.at[0, j], dev("z", d)).start()
        rc(gsv, gcv.at[y], gc_s.at[1, j], gc_r.at[1, j], dev("y", d)).start()
        return carry

    lax.fori_loop(0, N - 1, eighth, 0)

    key_rims = [
        (0, rc(agk.at[N - 1, pl.ds(HEADS, HEADS)], rimk.at[0], h_s.at[0], h_r.at[0], dev("z", 1))),
        (N - 1, rc(agk.at[0, pl.ds(0, HEADS)], rimk.at[1], h_s.at[2], h_r.at[2], dev("z", -1))),
    ]
    for end, copy in key_rims:
        pl.when(y == end)(copy.start)

    @pl.when(y > 0)
    def _():
        rimk[0] = agk[(y + N - 1) % N, pl.ds(HEADS, HEADS)]

    @pl.when(y < N - 1)
    def _():
        rimk[1] = agk[(y + 1) % N, pl.ds(0, HEADS)]


    def code_of(s, dest):
        return jnp.maximum(entry_of(s, dest) % 16 - 1, 0)

    def fill(dst_k, dst_v, zd, yd):
        for s in range(N):
            dst_k[s] = item(agk, s, code_of(z * N + s, zd * N + y))
            dst_v[s] = item(agv, s, code_of(s * N + y, z * N + yd))

    def bundle(j, carry):
        d = far_first(j)
        zd = (z + d) % N
        yd = (y + d) % N
        fill(sk.at[j], sv.at[j], zd, yd)
        rc(sk.at[j], rk.at[z], b_s.at[0, j], b_r.at[0, j], zd * N + y).start()
        rc(sv.at[j], rv.at[y], b_s.at[1, j], b_r.at[1, j], z * N + yd).start()
        return carry

    early = 3
    lax.fori_loop(0, early, bundle, 0)

    def eighth_wait(j, carry):
        d = far_first(j)
        zs = (z + N - d) % N
        ys = (y + N - d) % N
        rc(gsk, gck.at[zs], gc_s.at[0, j], gc_r.at[0, j], zs * N + y).wait_recv()
        rc(gsv, gcv.at[ys], gc_s.at[1, j], gc_r.at[1, j], z * N + ys).wait_recv()
        return carry

    def small(src_k, src_v, ss, rs, axis_k, axis_v):
        def start(j, carry):
            d = j + 1
            rc(src_k.at[pos[axis_k]], src_k.at[pos[axis_k]], ss.at[0, j], rs.at[0, j], dev(axis_k, d)).start()
            rc(src_v.at[pos[axis_v]], src_v.at[pos[axis_v]], ss.at[1, j], rs.at[1, j], dev(axis_v, d)).start()
            return carry

        lax.fori_loop(0, N - 1, start, 0)

    def small_wait(src_k, src_v, ss, rs, axis_k, axis_v):
        def wait(j, carry):
            d = N - 1 - j
            sl = (pos[axis_k] + d) % N
            rc(src_k.at[sl], src_k.at[sl], ss.at[0, j], rs.at[0, j], dev(axis_k, d)).wait_recv()
            sl = (pos[axis_v] + d) % N
            rc(src_v.at[sl], src_v.at[sl], ss.at[1, j], rs.at[1, j], dev(axis_v, d)).wait_recv()
            return carry

        lax.fori_loop(0, N - 1, wait, 0)

    lax.fori_loop(0, N - 1, eighth_wait, 0)
    gk[y] = gck[pick(y) // (2 * N)]
    gv[z] = gcv[pick(z) // 2 % N]
    small(gk, gv, gg_s, gg_r, "y", "z")
    lax.fori_loop(early, N - 1, bundle, 0)
    fill(rk.at[z], rv.at[y], z, y)
    for c_ in halo:
        c_.wait_recv()
    for end, copy in key_rims:
        pl.when(y == end)(copy.wait_recv)
    small_wait(gk, gv, gg_s, gg_r, "y", "z")

    def bundle_wait(j, carry):
        d = far_first(j)
        zs = (z + N - d) % N
        ys = (y + N - d) % N
        rc(sk.at[j], rk.at[zs], b_s.at[0, j], b_r.at[0, j], zs * N + y).wait_recv()
        rc(sv.at[j], rv.at[ys], b_s.at[1, j], b_r.at[1, j], z * N + ys).wait_recv()
        return carry

    scale = HD ** (-0.5)
    near = (3 + NGLOB) * BLK
    rows_by_cols = (((1,), (0,)), ((), ()))

    def dot(lhs, rhs, dims):
        return lax.dot_general(lhs, rhs, dims, preferred_element_type=F32)

    def over_pairs(one):
        def head(h, carry):
            cols = pl.ds(pl.multiple_of(h * HD, HD), HD)
            for b in range(2):
                one(h, b, 2 * h + b, pl.ds(b * BLK, BLK), cols)
            return carry

        lax.fori_loop(0, HEADS, head, 0)

    def first(h, b, i, rows, cols):
        trio = (rimk[0, h], agk[y, h], agk[y, HEADS + h], rimk[1, h])
        for j in range(3):
            ka1[i, pl.ds(j * BLK, BLK)] = trio[b + j]
        va1[i, pl.ds(0, 3 * BLK)] = winv[pl.ds(b * BLK, 3 * BLK), cols]
        for buf, glo in ((ka1, gk), (va1, gv)):
            for gi in range(NGLOB):
                buf[i, pl.ds((3 + gi) * BLK, BLK)] = glo[gi * HEADS + h]
        s = dot(q[rows, cols], ka1[i], ROWS_T) * scale
        key_id = lax.broadcasted_iota(jnp.int32, (BLK, near), 1)
        if b == 0:
            bad = (key_id < BLK) & (me == 0)
        else:
            bad = (key_id >= 2 * BLK) & (key_id < 3 * BLK) & (me == total - 1)
        s = jnp.where(bad, -jnp.inf, s)
        m = jnp.max(s, -1, keepdims=True)
        e = jnp.exp(s - m)
        dp = dot(g[rows, cols], va1[i], ROWS_T)
        s1[i], dp1[i] = e, dp
        stat[0, i] = m
        stat[1, i] = jnp.sum(e, -1, keepdims=True)
        stat[2, i] = jnp.sum(e * dp, -1, keepdims=True)

    over_pairs(first)
    lax.fori_loop(0, N - 1, bundle_wait, 0)

    def second(h, b, i, rows, cols):
        for r in range(NRAND):
            src = rbs[r, h, 2 * me + b] // 2
            ka2[i, pl.ds(r * BLK, BLK)] = rk[src // N, src % N]
            va2[i, pl.ds(r * BLK, BLK)] = rv[src % N, src // N]
        qb, gb = q[rows, cols], g[rows, cols]
        far = dot(qb, ka2[i], ROWS_T) * scale
        dp2 = dot(gb, va2[i], ROWS_T)
        m1 = stat[0, i]
        m = jnp.maximum(m1, jnp.max(far, -1, keepdims=True))
        shrink = jnp.exp(m1 - m)
        ef = jnp.exp(far - m)
        inv = 1.0 / (shrink * stat[1, i] + jnp.sum(ef, -1, keepdims=True))
        delta = (shrink * stat[2, i] + jnp.sum(ef * dp2, -1, keepdims=True)) * inv
        pf = ef * inv
        pf_low = pf.astype(BF16)
        dsf = (scale * pf * (dp2 - delta)).astype(BF16)
        p2[i], ds2[i] = pf_low, dsf
        stat[0, i] = shrink * inv
        stat[1, i] = delta
        for lhs, rhs, term in ((dsf, qb, termk), (pf_low, gb, termv)):
            t = dot(lhs, rhs, COLS_T)
            for r in range(NRAND):
                term[(h * NRAND + r) * 2 + b] = t[r * BLK : (r + 1) * BLK].astype(BF16)

    for h in range(HEADS):
        for b in range(2):
            second(h, b, 2 * h + b, pl.ds(b * BLK, BLK), pl.ds(h * HD, HD))

    def fill_back(dst_k, dst_v, zd, yd):
        for s in range(N):
            dst_k[s] = termk[entry_of(zd * N + s, me) // 16]
            dst_v[s] = termv[entry_of(s * N + yd, me) // 16]

    def back(j, carry):
        d = far_first(j)
        zd = (z + d) % N
        yd = (y + d) % N
        fill_back(rsk.at[j], rsv.at[j], zd, yd)
        rc(rsk.at[j], rrk.at[z], rb_s.at[0, j], rb_r.at[0, j], zd * N + y).start()
        rc(rsv.at[j], rrv.at[y], rb_s.at[1, j], rb_r.at[1, j], z * N + yd).start()
        return carry

    lax.fori_loop(0, N - 3, back, 0)
    fill_back(rrk.at[z], rrv.at[y], z, y)

    def third(h, b, i, rows, cols):
        qb, gb = q[rows, cols], g[rows, cols]
        pn = s1[i] * stat[0, i]
        pn_low = pn.astype(BF16)
        dsn = (scale * pn * (dp1[i] - stat[1, i])).astype(BF16)
        att[rows, cols] = (dot(pn_low, va1[i], rows_by_cols) + dot(p2[i], va2[i], rows_by_cols)).astype(BF16)
        dq[rows, cols] = (dot(dsn, ka1[i], rows_by_cols) + dot(ds2[i], ka2[i], rows_by_cols)).astype(BF16)
        for lhs, rhs, win, gacc in ((dsn, qb, wk, gak), (pn_low, gb, wv, gav)):
            t = dot(lhs, rhs, COLS_T)
            if b == 0:
                win[pl.ds(0, 3 * BLK), cols] = t[: 3 * BLK]
            else:
                win[pl.ds(BLK, 2 * BLK), cols] += t[: 2 * BLK]
                win[pl.ds(3 * BLK, BLK), cols] = t[2 * BLK : 3 * BLK]
            for gi in range(NGLOB):
                piece = t[(3 + gi) * BLK : (4 + gi) * BLK]
                if b == 0:
                    gacc[gi * HEADS + h] = piece
                else:
                    gacc[gi * HEADS + h] += piece

    over_pairs(third)
    for h in range(HEADS):
        hsk[0, h] = wk[pl.ds(0, BLK), pl.ds(h * HD, HD)].astype(BF16)
        hsk[1, h] = wk[pl.ds(3 * BLK, BLK), pl.ds(h * HD, HD)].astype(BF16)
    hsv[0] = wv[pl.ds(0, BLK)].astype(BF16)
    hsv[1] = wv[pl.ds(3 * BLK, BLK)].astype(BF16)
    gsbk[...] = gak[...].astype(BF16)
    gsbv[...] = gav[...].astype(BF16)
    grk[z] = gak[z].astype(BF16)
    grv[y] = gav[y].astype(BF16)

    def glob_back(j, carry):
        d = far_first(j)
        zd = (z + d) % N
        yd = (y + d) % N
        rc(gsbk.at[zd], grk.at[z], g1_s.at[0, j], g1_r.at[0, j], zd * N + y).start()
        rc(gsbv.at[yd], grv.at[y], g1_s.at[1, j], g1_r.at[1, j], z * N + yd).start()
        return carry

    def glob_back_wait(j, carry):
        d = far_first(j)
        zs = (z + N - d) % N
        ys = (y + N - d) % N
        rc(gsbk.at[zs], grk.at[zs], g1_s.at[0, j], g1_r.at[0, j], zs * N + y).wait_recv()
        rc(gsbv.at[ys], grv.at[ys], g1_s.at[1, j], g1_r.at[1, j], z * N + ys).wait_recv()
        return carry

    lax.fori_loop(0, N - 1, glob_back, 0)
    lax.fori_loop(N - 3, N - 1, back, 0)
    halo_back = [
        rc(hsv.at[0], hrv.at[1], hb_s.at[2], hb_r.at[2], left_seq),
        rc(hsv.at[1], hrv.at[0], hb_s.at[3], hb_r.at[3], right_seq),
    ]
    rim_back = [
        (0, rc(hsk.at[0], rimt.at[0], hb_s.at[0], hb_r.at[0], dev("z", -1))),
        (N - 1, rc(hsk.at[1], rimt.at[1], hb_s.at[1], hb_r.at[1], dev("z", 1))),
    ]
    for end, copy in rim_back:
        pl.when(y == end)(copy.start)
    for c_ in halo_back:
        c_.start()

    def back_wait(j, carry):
        d = far_first(j)
        zs = (z + N - d) % N
        ys = (y + N - d) % N
        rc(rsk.at[j], rrk.at[zs], rb_s.at[0, j], rb_r.at[0, j], zs * N + y).wait_recv()
        rc(rsv.at[j], rrv.at[ys], rb_s.at[1, j], rb_r.at[1, j], z * N + ys).wait_recv()
        return carry

    tile = 16
    arrivals = [(0, 4, 3, 5), (2, 6), (1, 7)]

    def partial(rel, wave):
        for buf, part, p in ((rrk, pk, y), (rrv, pv, z)):
            tgt = (p + rel) % N
            weight, rows_of = [], []
            for d in arrivals[wave]:
                if buf is rrk:
                    s = (z + N - d) % N
                    code = entry_of(z * N + tgt, s * N + y) % 16
                else:
                    s = (y + N - d) % N
                    code = entry_of(tgt * N + y, z * N + s) % 16
                rows_of.append(s)
                weight.append([jnp.where(code == i + 1, 1.0, 0.0).astype(F32) for i in range(ITEMS)])

            def rows_step(i, carry, buf=buf, part=part, tgt=tgt, weight=weight, rows_of=rows_of):
                rows = pl.ds(pl.multiple_of(i * tile, tile), tile)
                acc = [None if wave == 0 else part[tgt, c, rows] for c in range(ITEMS)]
                for s, ws in zip(rows_of, weight):
                    x = buf[s, tgt, rows].astype(F32)
                    for c in range(ITEMS):
                        w = x * ws[c]
                        acc[c] = w if acc[c] is None else acc[c] + w
                for c in range(ITEMS):
                    part[tgt, c, rows] = acc[c]
                return carry

            lax.fori_loop(0, BLK // tile, rows_step, 0)

    def step_loop(first_rel, stride, count, wave=2):
        def more(j, carry):
            partial((first_rel + stride * j) % N, wave)
            return carry

        lax.fori_loop(0, count, more, 0)

    def total_of(read):
        acc = read(0).astype(F32)
        for s in range(1, N):
            acc += read(s).astype(F32)
        return acc.astype(BF16)

    lax.fori_loop(0, 3, back_wait, 0)
    step_loop(0, 1, N, 0)
    lax.fori_loop(3, 5, back_wait, 0)
    step_loop(0, 1, N, 1)
    lax.fori_loop(0, N - 1, glob_back_wait, 0)
    g2k[y] = total_of(lambda s: grk[s])
    g2v[z] = total_of(lambda s: grv[s])
    small(g2k, g2v, g2_s, g2_r, "y", "z")
    for end, copy in rim_back:
        pl.when(y == end)(copy.wait_recv)

    @pl.when(y > 0)
    def _():
        pk[(y + N - 1) % N, pl.ds(HEADS, HEADS)] += hsk[0].astype(F32)

    @pl.when(y == 0)
    def _():
        pk[N - 1, pl.ds(HEADS, HEADS)] += rimt[0].astype(F32)

    @pl.when(y < N - 1)
    def _():
        pk[(y + 1) % N, pl.ds(0, HEADS)] += hsk[1].astype(F32)

    @pl.when(y == N - 1)
    def _():
        pk[0, pl.ds(0, HEADS)] += rimt[1].astype(F32)

    lax.fori_loop(5, N - 1, back_wait, 0)

    rs_index = {key: i for i, key in enumerate(RS)}

    def rs_copy(arr, i):
        f, s = RS[i]
        return rc(rsend.at[arr, i], rrecv.at[arr, i], rs_s.at[arr, i], rs_r.at[arr, i],
                  dev(("y", "z")[arr], FLOWS[f][0]))

    def rs_send(f, s):
        dr, c, hops = FLOWS[f]
        i = rs_index[(f, s)]
        for arr, part, p in ((0, pk, y), (1, pv, z)):
            tgt = (p + dr * (hops - s + 1) + N) % N
            x = part[tgt, pl.ds(c * HEADS, HEADS)]
            if s > 1:
                j = rs_index[(f, s - 1)]
                rs_copy(arr, j).wait_recv()
                x = x + rrecv[arr, j].astype(F32)
            rsend[arr, i] = x.astype(BF16)
            rs_copy(arr, i).start()

    step_loop(3, 1, 3)
    for f in range(4):
        rs_send(f, 1)
    step_loop(2, 4, 2)
    small_wait(g2k, g2v, g2_s, g2_r, "y", "z")
    g3k[z] = total_of(lambda s: g2k[s])
    g3v[y] = total_of(lambda s: g2v[s])
    small(g3k, g3v, g3_s, g3_r, "z", "y")
    for f in range(4):
        rs_send(f, 2)
    step_loop(7, 1, 3)
    for f in range(4):
        rs_send(f, 3)
    for f in range(2):
        rs_send(f, 4)
    for c_ in halo_back:
        c_.wait_recv()
    small_wait(g3k, g3v, g3_s, g3_r, "z", "y")

    parts = ((0, pk, y, wk, None, g3k, dk), (1, pv, z, wv, hrv, g3v, dv))
    for arr, part, p, win, hr, g3, out in parts:
        for b in range(2):
            mine = [jnp.where(gblk[gi] == me * 2 + b, 1.0, 0.0).astype(F32) for gi in range(NGLOB)]
            for h in range(HEADS):
                cols = pl.ds(h * HD, HD)
                x = part[p, b * HEADS + h] + win[pl.ds((1 + b) * BLK, BLK), cols]
                if hr is not None:
                    x += hr[b, :, cols].astype(F32)
                for gi in range(NGLOB):
                    x += g3[gi * HEADS + h].astype(F32) * mine[gi]
                part[p, b * HEADS + h] = x
    for f in (2, 3, 0, 1):
        i = rs_index[(f, FLOWS[f][2])]
        b = FLOWS[f][1]
        for arr, part, p, win, hr, g3, out in parts:
            rs_copy(arr, i).wait_recv()
            for h in range(HEADS):
                x = part[p, b * HEADS + h] + rrecv[arr, i, h].astype(F32)
                if f < 2:
                    out[pl.ds(b * BLK, BLK), pl.ds(h * HD, HD)] = x.astype(BF16)
                else:
                    part[p, b * HEADS + h] = x

    for arr in (0, 1):
        for i in range(len(AG)):
            ag_copy(arr, i).wait_send()
        for i in range(len(RS)):
            rs_copy(arr, i).wait_send()
    for c_ in halo + halo_back:
        c_.wait_send()
    for end, copy in key_rims + rim_back:
        pl.when(y == end)(copy.wait_send)

    def drain(j, carry):
        for a, (bk, bv) in ((b_s, (sk, sv)), (rb_s, (rsk, rsv))):
            rc(bk.at[j], rk.at[z], a.at[0, j], b_r.at[0, j], me).wait_send()
            rc(bv.at[j], rv.at[y], a.at[1, j], b_r.at[1, j], me).wait_send()
        for a, (bk, bv), (ik, iv) in (
            (gg_s, (gk, gv), (y, z)),
            (g2_s, (g2k, g2v), (y, z)),
            (g3_s, (g3k, g3v), (z, y)),
        ):
            rc(bk.at[ik], bk.at[ik], a.at[0, j], gg_r.at[0, j], me).wait_send()
            rc(bv.at[iv], bv.at[iv], a.at[1, j], gg_r.at[1, j], me).wait_send()
        rc(gsbk.at[z], grk.at[z], g1_s.at[0, j], g1_r.at[0, j], me).wait_send()
        rc(gsbv.at[y], grv.at[y], g1_s.at[1, j], g1_r.at[1, j], me).wait_send()
        rc(gsk, gck.at[z], gc_s.at[0, j], gc_r.at[0, j], me).wait_send()
        rc(gsv, gcv.at[y], gc_s.at[1, j], gc_r.at[1, j], me).wait_send()
        return carry

    lax.fori_loop(0, N - 1, drain, 0)


def settle(*refs):
    for src, dst in zip(refs[:4], refs[4:]):
        dst[...] = src[...]


def body(queries, keys, values, out_grad, random_blocks, global_blocks):
    lists = random_blocks.transpose(1, 0, 2)
    full = jax.ShapeDtypeStruct(queries.shape, BF16)
    vm, dma = pltpu.VMEM, pltpu.SemaphoreType.DMA
    bund = lambda n, slots: vm((n, slots, BLK, HD), BF16)
    near, far = (3 + NGLOB) * BLK, NRAND * BLK
    small = vm((N, BLK, HD), BF16)
    scratch = [
        vm(queries.shape, BF16), vm(queries.shape, BF16),
        vm(lists.shape, jnp.int32), pltpu.SMEM(lists.shape, jnp.int32),
        vm((N * N, 2 * N * N), jnp.int32), pltpu.SMEM((N * N, 2 * N * N), jnp.int32),
        vm((BLK, HD), BF16), vm((BLK, HD), BF16), small, small,
        vm((N, ITEMS, BLK, HD), BF16), vm((N, ITEMS, BLK, HD), BF16),
        vm((4 * BLK, HEADS * HD), BF16),
        bund(N - 1, N), bund(N - 1, N), bund(N, N), bund(N, N),
        vm((N, BLK, HD), BF16), vm((N, BLK, HD), BF16),
        vm((ITEMS, near, HD), BF16), vm((ITEMS, near, HD), BF16),
        vm((ITEMS, far, HD), BF16), vm((ITEMS, far, HD), BF16),
        vm((ITEMS, BLK, near), F32), vm((ITEMS, BLK, near), F32),
        vm((ITEMS, BLK, far), BF16), vm((ITEMS, BLK, far), BF16),
        vm((3, ITEMS, BLK, 1), F32), vm((2, HEADS, BLK, HD), BF16), vm((2, HEADS, BLK, HD), BF16),
        small, small, small, small,
        vm((24, BLK, HD), BF16), vm((24, BLK, HD), BF16),
        vm((4 * BLK, HEADS * HD), F32), vm((4 * BLK, HEADS * HD), F32),
        vm((N, BLK, HD), F32), vm((N, BLK, HD), F32),
        vm((2, HEADS, BLK, HD), BF16), vm((2, BLK, HEADS * HD), BF16),
        vm((2, BLK, HEADS * HD), BF16),
        bund(N - 1, N), bund(N - 1, N), bund(N, N), bund(N, N),
        vm((N, ITEMS, BLK, HD), F32), vm((N, ITEMS, BLK, HD), F32),
        vm((N, BLK, HD), BF16), vm((N, BLK, HD), BF16),
        vm((N, BLK, HD), BF16), vm((N, BLK, HD), BF16),
        vm((2, len(RS), HEADS, BLK, HD), BF16), vm((2, len(RS), HEADS, BLK, HD), BF16),
        dma((2, N - 1)), dma((2, N - 1)),
        dma, dma((2, N - 1)), dma((2, N - 1)), dma((2 * ITEMS + 6,)), dma((2, len(AG))), dma((2, len(AG))), dma((4,)), dma((4,)),
        dma((2, N - 1)), dma((2, N - 1)), dma((2, N - 1)), dma((2, N - 1)),
        dma((4,)), dma((4,)), dma((2, N - 1)), dma((2, N - 1)),
        dma((2, N - 1)), dma((2, N - 1)), dma((2, N - 1)), dma((2, N - 1)),
        dma((2, len(RS))), dma((2, len(RS))),
    ]
    spec = pl.BlockSpec(memory_space=pltpu.VMEM)
    smem = pl.BlockSpec(memory_space=pltpu.SMEM)
    outs = pl.pallas_call(
        kernel,
        out_shape=(full,) * 4,
        in_specs=[smem] + [pl.BlockSpec(memory_space=pltpu.MemorySpace.HBM)] * 5,
        out_specs=(spec,) * 4,
        scratch_shapes=scratch,
        compiler_params=pltpu.CompilerParams(collective_id=0, has_side_effects=True),
    )(global_blocks, lists, queries, keys, values, out_grad)
    return pl.pallas_call(
        settle,
        out_shape=(full,) * 4,
        in_specs=[spec] * 4,
        out_specs=(spec,) * 4,
    )(*outs)


def solution(mesh):
    wide = P(("dp", "seq"), "heads")
    return jax.shard_map(
        body,
        mesh=mesh,
        in_specs=(wide, wide, wide, wide, P(("dp", "heads"), None, None), P("dp")),
        out_specs=(wide,) * 4,
        check_vma=False,
    )
```
